32 devices in a mesh: dp: 8 (over z, core), tensor: 4 (over y, x).
Axes of the slice: x: 2, y: 2, z: 4, core: 2. Of those that a mesh axis runs over, the one named last changes fastest.
Arguments:
- image_tokens: bfloat16 [8192, 1536], P(('dp', 'tensor')), may hold values from -6 to 6
- text_tokens: bfloat16 [1024, 1536], P(('dp', 'tensor')), may hold values from -6 to 6
- conditioning: float32 [6, 1536], replicated, may hold values from -6 to 6
- slot_sequence: int32 [8], P('dp'), may hold values from 0 to 5, as said below
- rank_counts: int32 [8], P('dp'), may hold values from 0 to 1, as said below
- projection: bfloat16 [2, 2, 1536, 4608], P(None, None, 'dp', 'tensor'), may hold values from -0.15625 to 0.15625
- recombine: bfloat16 [2, 2, 1536, 1536], P(None, None, 'dp', 'tensor'), may hold values from -1.25 to 1.25
- expansion: bfloat16 [2, 2, 1536, 6144], P(None, None, 'dp', 'tensor'), may hold values from -0.15625 to 0.15625
- contraction: bfloat16 [2, 2, 1536, 6144], P(None, None, 'dp', 'tensor'), may hold values from -0.15625 to 0.15625
- modulation: bfloat16 [2, 2, 1536, 9216], P(None, None, ('dp', 'tensor')), may hold values from -0.15625 to 0.15625
- biases: bfloat16 [2, 2, 21504], P(None, None, ('dp', 'tensor')), may hold values from -1.796875 to 1.796875
- cotangent_image: bfloat16 [8192, 1536], P(('dp', 'tensor')), may hold values from -6 to 6
- cotangent_text: bfloat16 [1024, 1536], P(('dp', 'tensor')), may hold values from -6 to 6
Outputs:
- image_output: bfloat16 [8192, 1536], P(('dp', 'tensor'))
- text_output: bfloat16 [1024, 1536], P(('dp', 'tensor'))
- image_grad: float32 [8192, 1536], P(('dp', 'tensor'))
- text_grad: float32 [1024, 1536], P(('dp', 'tensor'))
- projection_grad: float32 [2, 2, 1536, 4608], P(None, None, 'dp', 'tensor')
- recombine_grad: float32 [2, 2, 1536, 1536], P(None, None, 'dp', 'tensor')
- expansion_grad: float32 [2, 2, 1536, 6144], P(None, None, 'dp', 'tensor')
- contraction_grad: float32 [2, 2, 1536, 6144], P(None, None, 'dp', 'tensor')
- modulation_grad: float32 [2, 2, 1536, 9216], P(None, None, ('dp', 'tensor'))
- biases_grad: float32 [2, 2, 21504], P(None, None, ('dp', 'tensor'))
The draws below stay inside these ranges and needn't reach their ends.
Inputs may be any that keep to these rules, and one draw needn't show every extreme that they name: `rank_counts`: each dp rank's count is its number of live slots, which come first among its 1; the counts sum to 6 and at least one rank holds 1. `slot_sequence`: each of the 6 sequences is named by exactly one live slot; an empty slot names any sequence.
All inputs are finite; a program needn't handle non-finite values.
Results may differ from the reference program's by a relative error of at most 0.03.
Values may be sent and summed in bfloat16 or wider, within the bound.
A program may use at most 320 MiB of HBM per device.

```python
import jax
import jax.numpy as jnp
from jax import lax

D = 1536
HEADS = 24
HEAD_DIM = 64
FF = 6144
LAYERS = 2
IMG = 1024
TXT = 128
CAP = 1
SLOTS = 8
NSEQ = 6
NB = 21504


def slot_layout(key):
    rank_total = SLOTS // CAP
    empty_slots = SLOTS // 4
    priority = jax.random.permutation(jax.random.fold_in(key, 101), SLOTS).astype(jnp.int32)
    protected = jax.random.randint(jax.random.fold_in(key, 102), (), 0, rank_total, dtype=jnp.int32)
    owners = jnp.arange(SLOTS, dtype=jnp.int32) // CAP
    priority = priority + (owners == protected).astype(jnp.int32) * SLOTS
    ordering = jnp.argsort(priority, stable=True)
    dropped = jnp.zeros((SLOTS,), jnp.int32).at[ordering[:empty_slots]].set(1)
    counts = (CAP - jnp.sum(dropped.reshape(rank_total, CAP), axis=1)).astype(jnp.int32)
    places = jnp.arange(SLOTS, dtype=jnp.int32) % CAP
    live_slot = (places < counts[owners]).astype(jnp.int32)
    position = jnp.clip(jnp.cumsum(live_slot) - 1, 0, NSEQ - 1).astype(jnp.int32)
    shuffled = jax.random.permutation(jax.random.fold_in(key, 103), NSEQ).astype(jnp.int32)
    filler = jax.random.randint(jax.random.fold_in(key, 104), (SLOTS,), 0, NSEQ, dtype=jnp.int32)
    sequence = jnp.where(live_slot == 1, shuffled[position], filler).astype(jnp.int32)
    return (counts, sequence)


def draw_rank_counts(key, part):
    return slot_layout(key)[0]


def draw_slot_sequence(key, part):
    return slot_layout(key)[1]


def steps_of(stream_key, extent, cuts, smallest, largest):
    loudness, own = 1.0, jax.random.fold_in(stream_key, 6)
    for dim, shards_of in cuts:
        draws = jnp.exp(jax.random.uniform(jax.random.fold_in(own, dim), (shards_of,), jnp.float32, smallest / len(cuts), largest / len(cuts)))
        loudness = loudness * jnp.repeat(draws, extent[dim] // shards_of).reshape([-1 if axis == dim else 1 for axis in range(len(extent))])
    return loudness


def normal_values(stream_key, dims, width, most, cuts=(), kind=jnp.bfloat16):
    gain = steps_of(stream_key, dims, cuts, -0.22, 0.18) if cuts else 1.0
    values = jax.random.normal(stream_key, dims, jnp.float32) * width * gain
    return jnp.minimum(jnp.maximum(values, -most), most).astype(kind)


def setup_inputs(seed: int = 0) -> dict:
    keys = jax.random.split(jax.random.key(seed), 14)
    image_tokens = normal_values(keys[0], (SLOTS * IMG, D), 1.0, 6.0, ((0, 32),))
    text_tokens = normal_values(keys[1], (SLOTS * TXT, D), 1.0, 6.0, ((0, 32),))
    conditioning = normal_values(keys[2], (NSEQ, D), 1.0, 6.0, (), jnp.float32)
    slot_sequence = draw_slot_sequence(jax.random.fold_in(keys[13], 71), 0)
    rank_counts = draw_rank_counts(jax.random.fold_in(keys[13], 71), 0)
    projection = normal_values(keys[5], (LAYERS, 2, D, 3 * D), D ** -0.5, 0.15625, ((2, 8), (3, 4)))
    recombine = normal_values(keys[6], (LAYERS, 2, D, D), (D // 64) ** -0.5, 1.25, ((2, 8), (3, 4)))
    expansion = normal_values(keys[7], (LAYERS, 2, D, FF), D ** -0.5, 0.15625, ((2, 8), (3, 4)))
    contraction = normal_values(keys[8], (LAYERS, 2, D, FF), (FF // 4) ** -0.5, 0.15625, ((2, 8), (3, 4)))
    modulation = normal_values(keys[9], (LAYERS, 2, D, 6 * D), D ** -0.5, 0.15625, ((2, 32),))
    biases = normal_values(keys[10], (LAYERS, 2, NB), 0.3, 1.796875, ((2, 32),))
    cotangent_image = normal_values(keys[11], (SLOTS * IMG, D), 1.0, 6.0, ((0, 32),))
    cotangent_text = normal_values(keys[12], (SLOTS * TXT, D), 1.0, 6.0, ((0, 32),))
    return dict(image_tokens=image_tokens, text_tokens=text_tokens, conditioning=conditioning, slot_sequence=slot_sequence, rank_counts=rank_counts, projection=projection, recombine=recombine, expansion=expansion, contraction=contraction, modulation=modulation, biases=biases, cotangent_image=cotangent_image, cotangent_text=cotangent_text)


highest = lax.Precision.HIGHEST

@jax.custom_vjp
def low(v):
    return lax.optimization_barrier(v.astype(jnp.bfloat16)).astype(jnp.float32)

@jax.custom_vjp
def low_back(v):
    return v

def low_keep(v):
    return (low(v), None)

def low_pass(kept, grad):
    return (grad,)

def back_keep(v):
    return (v, None)

def back_low(kept, grad):
    return (low(grad),)
low.defvjp(low_keep, low_pass)
low_back.defvjp(back_keep, back_low)

def layer_norm(values):
    average = lax.optimization_barrier(jnp.mean(values, -1, keepdims=True))
    centred = values - average
    spread = lax.optimization_barrier(jnp.mean(centred * centred, -1, keepdims=True))
    return centred * lax.rsqrt(spread + 1e-06)

def matmul(operand, factor):
    return jnp.dot(operand, factor, precision=highest)

def slot_block(parameters, image_rows, text_rows, modulations):
    projection, recombine, expansion, contraction, biases = parameters
    streams = [image_rows, text_rows]
    for tier_index in range(LAYERS):
        pieces = []
        for stream in range(2):
            shifts = modulations[tier_index, stream].reshape(6, D)
            bias_row = biases[tier_index, stream]
            normed = low(layer_norm(streams[stream]) * (1.0 + shifts[1]) + shifts[0])
            projected = matmul(normed, projection[tier_index, stream]).reshape(-1, HEADS, 3, HEAD_DIM)
            queries = projected[:, :, 0] + bias_row[6 * D:7 * D].reshape(HEADS, HEAD_DIM)
            key_rows = projected[:, :, 1]
            values = projected[:, :, 2] + bias_row[7 * D:8 * D].reshape(HEADS, HEAD_DIM)
            pieces.append((queries, key_rows, values))
        queries = low_back(low(jnp.concatenate([pieces[0][0], pieces[1][0]], 0)))
        key_rows = low_back(low(jnp.concatenate([pieces[0][1], pieces[1][1]], 0)))
        values = low_back(low(jnp.concatenate([pieces[0][2], pieces[1][2]], 0)))
        scores = low_back(jnp.einsum('qhe,khe->hqk', queries, key_rows, precision=highest) * HEAD_DIM ** (-0.5))
        weights = low(jax.nn.softmax(scores, -1))
        attended = jnp.einsum('hqk,khe->qhe', weights, values, precision=highest).reshape(-1, D)
        attended = low_back(low(attended))
        updated = []
        for stream in range(2):
            shifts = modulations[tier_index, stream].reshape(6, D)
            bias_row = biases[tier_index, stream]
            row_part = attended[:IMG] if stream == 0 else attended[IMG:]
            branch = low_back(jnp.einsum('rc,oc->ro', row_part, recombine[tier_index, stream], precision=highest)) + bias_row[8 * D:9 * D]
            middle = streams[stream] + shifts[2] * branch
            normed = low(layer_norm(middle) * (1.0 + shifts[4]) + shifts[3])
            preact = low_back(matmul(normed, expansion[tier_index, stream]) + bias_row[9 * D:9 * D + FF])
            activated = low(jax.nn.gelu(preact, approximate=True))
            branch = low_back(jnp.einsum('rf,of->ro', activated, contraction[tier_index, stream], precision=highest)) + bias_row[9 * D + FF:]
            updated.append(middle + shifts[5] * branch)
        streams = updated
    return (streams[0], streams[1])

def reference(image_tokens, text_tokens, conditioning, slot_sequence, rank_counts, projection, recombine, expansion, contraction, modulation, biases, cotangent_image, cotangent_text):
    slot_place = jnp.arange(SLOTS, dtype=jnp.int32)
    live_mask = (slot_place % CAP < rank_counts[slot_place // CAP]).astype(jnp.float32)
    onehot = (slot_sequence[:, None] == jnp.arange(NSEQ, dtype=jnp.int32)[None, :]).astype(jnp.float32)
    silu_values = jax.nn.silu(conditioning)
    checked = jax.checkpoint(slot_block)

    def forward(image_rows, text_rows, weight_qkv, weight_out, weight_up, weight_down, weight_mod, bias_all):
        shift_table = jnp.einsum('nd,lsdm->lsnm', silu_values, weight_mod, precision=highest) + bias_all[:, :, None, :6 * D]
        per_slot = jnp.einsum('pn,lsnm->plsm', onehot, shift_table, precision=highest)
        parameters = (weight_qkv, weight_out, weight_up, weight_down, bias_all)

        def run_slot(entry):
            return checked(parameters, entry[0], entry[1], entry[2])
        image_out, text_out = lax.map(run_slot, (image_rows.reshape(SLOTS, IMG, D), text_rows.reshape(SLOTS, TXT, D), per_slot))
        image_out = (image_out * live_mask[:, None, None]).reshape(SLOTS * IMG, D)
        text_out = (text_out * live_mask[:, None, None]).reshape(SLOTS * TXT, D)
        return (image_out, text_out)
    outputs, pullback = jax.vjp(forward, image_tokens.astype(jnp.float32), text_tokens.astype(jnp.float32), projection.astype(jnp.float32), recombine.astype(jnp.float32), expansion.astype(jnp.float32), contraction.astype(jnp.float32), modulation.astype(jnp.float32), biases.astype(jnp.float32))
    gradients = pullback((cotangent_image.astype(jnp.float32), cotangent_text.astype(jnp.float32)))
    return (outputs[0].astype(jnp.bfloat16), outputs[1].astype(jnp.bfloat16), gradients[0], gradients[1], gradients[2], gradients[3], gradients[4], gradients[5], gradients[6], gradients[7])
```

```python
import functools
import math

import jax
import jax.numpy as jnp
from jax import lax
from jax.experimental import pallas as pl
from jax.experimental.pallas import tpu as pltpu
from jax.sharding import PartitionSpec as P

D = 1536
HEADS = 24
HEAD_DIM = 64
FF = 6144
LAYERS = 2

highest = lax.Precision.HIGHEST
contract_columns = (((1,), (1,)), ((), ()))
contract_rows = (((0,), (0,)), ((), ()))
SCALE = HEAD_DIM ** (-0.5)
EXPONENT = SCALE * math.log2(math.e)


def normalize(values):
    average = jnp.mean(values, -1, keepdims=True)
    centred = values - average
    spread = jnp.mean(centred * centred, -1, keepdims=True)
    return centred * lax.rsqrt(spread + 1e-06)


def modulate(values, shifts, scales):
    return normalize(values) * (1.0 + scales) + shifts


def gelu_tanh(values):
    return jax.nn.gelu(values, approximate=True)


def exchange(values, axis, step):
    size = lax.axis_size(axis)
    return lax.ppermute(values, axis, [(rank, rank ^ step) for rank in range(size)])


def gather_parts(values, axis):
    return [values] + [exchange(values, axis, step) for step in range(1, lax.axis_size(axis))]


def gather_rows(values, axis):
    return jnp.concatenate(gather_parts(values, axis), axis=0)


def scatter_rows(values, axis):
    size = lax.axis_size(axis)
    rows = values.shape[0] // size
    total = values[:rows].astype(jnp.float32)
    for step in range(1, size):
        total = total + exchange(values[step * rows : (step + 1) * rows], axis, step).astype(
            jnp.float32
        )
    return total


def sum_over(values, axis):
    total = values
    for step in range(1, lax.axis_size(axis)):
        total = total + exchange(values, axis, step)
    return total


def row_block(rows):
    for block in (384, 256, 128):
        if rows % block == 0:
            return block
    return rows


def attend_kernel(heads, block, columns_ref, out_ref, log_ref):
    rows = columns_ref.shape[0]
    for head in range(heads):
        base = head * 3 * HEAD_DIM
        keys = columns_ref[:, base + HEAD_DIM : base + 2 * HEAD_DIM]
        values = columns_ref[:, base + 2 * HEAD_DIM : base + 3 * HEAD_DIM]

        def step(index, carry):
            place = pl.ds(pl.multiple_of(index * block, block), block)
            queries = columns_ref[place, base : base + HEAD_DIM]
            scores = lax.dot_general(
                queries, keys, contract_columns, preferred_element_type=jnp.float32
            )
            row_max = jnp.max(scores, -1, keepdims=True)
            weights = jnp.exp2((scores - row_max) * EXPONENT)
            totals = jnp.sum(weights, -1, keepdims=True)
            output = jnp.dot(
                weights.astype(jnp.bfloat16), values, preferred_element_type=jnp.float32
            )
            out_ref[place, head * HEAD_DIM : (head + 1) * HEAD_DIM] = (output / totals).astype(
                jnp.bfloat16
            )
            log_ref[place, head : head + 1] = row_max * EXPONENT + jnp.log2(totals)
            return carry

        lax.fori_loop(0, rows // block, step, 0)


def attend(columns, heads):
    rows = columns.shape[0]
    return pl.pallas_call(
        functools.partial(attend_kernel, heads, row_block(rows)),
        out_shape=(
            jax.ShapeDtypeStruct((rows, heads * HEAD_DIM), jnp.bfloat16),
            jax.ShapeDtypeStruct((rows, 128), jnp.float32),
        ),
        cost_estimate=pl.CostEstimate(
            flops=heads * rows * rows * HEAD_DIM * 4,
            bytes_accessed=columns.size * 3,
            transcendentals=heads * rows * rows,
        ),
        name="attend",
    )(columns)


def attend_back_kernel(
    heads, block, columns_ref, out_ref, log_ref, grad_ref, result_ref, key_acc, value_acc
):
    rows = columns_ref.shape[0]
    for head in range(heads):
        base = head * 3 * HEAD_DIM
        part = slice(head * HEAD_DIM, (head + 1) * HEAD_DIM)
        keys = columns_ref[:, base + HEAD_DIM : base + 2 * HEAD_DIM]
        values = columns_ref[:, base + 2 * HEAD_DIM : base + 3 * HEAD_DIM]
        key_acc[...] = jnp.zeros_like(key_acc)
        value_acc[...] = jnp.zeros_like(value_acc)

        def step(index, carry):
            place = pl.ds(pl.multiple_of(index * block, block), block)
            queries = columns_ref[place, base : base + HEAD_DIM]
            grad_out = grad_ref[place, part]
            inner = jnp.sum(
                grad_out.astype(jnp.float32) * out_ref[place, part].astype(jnp.float32),
                -1,
                keepdims=True,
            )
            scores = lax.dot_general(
                queries, keys, contract_columns, preferred_element_type=jnp.float32
            )
            weights = jnp.exp2(scores * EXPONENT - log_ref[place, head : head + 1])
            grad_weights = lax.dot_general(
                grad_out, values, contract_columns, preferred_element_type=jnp.float32
            )
            grad_scores = (weights * (grad_weights - inner)).astype(jnp.bfloat16)
            result_ref[place, base : base + HEAD_DIM] = (
                jnp.dot(grad_scores, keys, preferred_element_type=jnp.float32) * SCALE
            ).astype(jnp.bfloat16)
            key_acc[...] += lax.dot_general(
                grad_scores, queries, contract_rows, preferred_element_type=jnp.float32
            )
            value_acc[...] += lax.dot_general(
                weights.astype(jnp.bfloat16),
                grad_out,
                contract_rows,
                preferred_element_type=jnp.float32,
            )
            return carry

        lax.fori_loop(0, rows // block, step, 0)
        result_ref[:, base + HEAD_DIM : base + 2 * HEAD_DIM] = (key_acc[...] * SCALE).astype(
            jnp.bfloat16
        )
        result_ref[:, base + 2 * HEAD_DIM : base + 3 * HEAD_DIM] = value_acc[...].astype(
            jnp.bfloat16
        )


def attend_back(columns, output, logsum, grad_output, heads):
    rows = columns.shape[0]
    return pl.pallas_call(
        functools.partial(attend_back_kernel, heads, row_block(rows)),
        out_shape=jax.ShapeDtypeStruct(columns.shape, jnp.bfloat16),
        scratch_shapes=[
            pltpu.VMEM((rows, HEAD_DIM), jnp.float32),
            pltpu.VMEM((rows, HEAD_DIM), jnp.float32),
        ],
        cost_estimate=pl.CostEstimate(
            flops=heads * rows * rows * HEAD_DIM * 10,
            bytes_accessed=columns.size * 6,
            transcendentals=heads * rows * rows,
        ),
        name="attend_back",
    )(columns, output, logsum, grad_output)


def column_bias(query_bias, value_bias, heads):
    query_part = query_bias.reshape(heads, HEAD_DIM)
    value_part = value_bias.reshape(heads, HEAD_DIM)
    return jnp.stack([query_part, jnp.zeros_like(query_part), value_part], axis=1).reshape(-1)


def layer_biases(bias_layer, tensor_rank, width_local, hidden_local):
    query_bias = lax.dynamic_slice_in_dim(
        bias_layer, 6 * D + tensor_rank * width_local, width_local, 1
    )
    value_bias = lax.dynamic_slice_in_dim(
        bias_layer, 7 * D + tensor_rank * width_local, width_local, 1
    )
    out_bias = bias_layer[:, 8 * D : 9 * D]
    hidden_bias = lax.dynamic_slice_in_dim(
        bias_layer, 9 * D + tensor_rank * hidden_local, hidden_local, 1
    )
    last_bias = bias_layer[:, 9 * D + FF :]
    return (query_bias, value_bias, out_bias, hidden_bias, last_bias)


def forward_layer(states, weights, pieces, shifts, heads_local):
    query_bias, value_bias, out_bias, hidden_bias, last_bias = pieces
    joined = [
        gather_rows(
            modulate(states[stream], shifts[stream][0], shifts[stream][1]).astype(jnp.bfloat16),
            "tensor",
        )
        for stream in range(2)
    ]
    columns = jnp.concatenate(
        [
            (
                jnp.dot(joined[stream], weights[0][stream], preferred_element_type=jnp.float32)
                + column_bias(query_bias[stream], value_bias[stream], heads_local)
            ).astype(jnp.bfloat16)
            for stream in range(2)
        ]
    )
    attended, logsum = attend(columns, heads_local)
    split = joined[0].shape[0]
    out_rows = [attended[:split], attended[split:]]
    branch_attend = [
        scatter_rows(
            lax.dot_general(
                out_rows[stream],
                weights[1][stream],
                contract_columns,
                preferred_element_type=jnp.float32,
            ).astype(jnp.bfloat16),
            "tensor",
        )
        + out_bias[stream]
        for stream in range(2)
    ]
    middle = [states[stream] + shifts[stream][2] * branch_attend[stream] for stream in range(2)]
    joined_feed = [
        gather_rows(
            modulate(middle[stream], shifts[stream][3], shifts[stream][4]).astype(jnp.bfloat16),
            "tensor",
        )
        for stream in range(2)
    ]
    preact = [
        jnp.dot(joined_feed[stream], weights[2][stream], preferred_element_type=jnp.float32)
        + hidden_bias[stream]
        for stream in range(2)
    ]
    activated = [gelu_tanh(preact[stream]).astype(jnp.bfloat16) for stream in range(2)]
    branch_feed = [
        scatter_rows(
            lax.dot_general(
                activated[stream],
                weights[3][stream],
                contract_columns,
                preferred_element_type=jnp.float32,
            ).astype(jnp.bfloat16),
            "tensor",
        )
        + last_bias[stream]
        for stream in range(2)
    ]
    result = [middle[stream] + shifts[stream][5] * branch_feed[stream] for stream in range(2)]
    record = (
        states,
        joined,
        columns,
        attended,
        logsum,
        branch_attend,
        middle,
        joined_feed,
        preact,
        activated,
        branch_feed,
    )
    return (record, result)


def scatter_weights(grads):
    return [
        lax.psum_scatter(grad.astype(jnp.bfloat16), "dp", scatter_dimension=0, tiled=True).astype(
            jnp.float32
        )
        for grad in grads
    ]


def backward_layer(gradients, record, weights, shifts, heads_local):
    (
        states,
        joined,
        columns,
        attended,
        logsum,
        branch_attend,
        middle,
        joined_feed,
        preact,
        activated,
        branch_feed,
    ) = record
    split = joined[0].shape[0]
    out_rows = [attended[:split], attended[split:]]
    grad_branch = [shifts[stream][5] * gradients[stream] for stream in range(2)]
    gate_feed = [jnp.sum(gradients[stream] * branch_feed[stream], 0) for stream in range(2)]
    branch_rows = [
        gather_rows(grad_branch[stream].astype(jnp.bfloat16), "tensor") for stream in range(2)
    ]
    grad_contraction = scatter_weights(
        [
            lax.dot_general(
                branch_rows[stream],
                activated[stream],
                contract_rows,
                preferred_element_type=jnp.float32,
            )
            for stream in range(2)
        ]
    )
    grad_preact = []
    for stream in range(2):
        grad_activated = jnp.dot(
            branch_rows[stream], weights[3][stream], preferred_element_type=jnp.float32
        )
        gelu_back = jax.vjp(gelu_tanh, preact[stream])[1]
        grad_preact.append(gelu_back(grad_activated)[0].astype(jnp.bfloat16))
    hidden_sums = [jnp.sum(grad_preact[stream], 0, dtype=jnp.float32) for stream in range(2)]
    summed = [
        scatter_rows(
            lax.dot_general(
                grad_preact[stream],
                weights[2][stream],
                contract_columns,
                preferred_element_type=jnp.float32,
            ).astype(jnp.bfloat16),
            "tensor",
        )
        for stream in range(2)
    ]
    grad_expansion = scatter_weights(
        [
            lax.dot_general(
                joined_feed[stream],
                grad_preact[stream],
                contract_rows,
                preferred_element_type=jnp.float32,
            )
            for stream in range(2)
        ]
    )
    grad_middle, shift_feed, scale_feed = ([], [], [])
    for stream in range(2):
        shift_back = jax.vjp(modulate, middle[stream], shifts[stream][3], shifts[stream][4])[1]
        back_rows, back_shift, back_scale = shift_back(summed[stream])
        grad_middle.append(gradients[stream] + back_rows)
        shift_feed.append(back_shift)
        scale_feed.append(back_scale)
    grad_attend = [shifts[stream][2] * grad_middle[stream] for stream in range(2)]
    gate_attend = [jnp.sum(grad_middle[stream] * branch_attend[stream], 0) for stream in range(2)]
    attend_rows = [
        gather_rows(grad_attend[stream].astype(jnp.bfloat16), "tensor") for stream in range(2)
    ]
    grad_heads = jnp.concatenate(
        [
            jnp.dot(
                attend_rows[stream], weights[1][stream], preferred_element_type=jnp.float32
            ).astype(jnp.bfloat16)
            for stream in range(2)
        ]
    )
    grad_recombine = scatter_weights(
        [
            lax.dot_general(
                attend_rows[stream],
                out_rows[stream],
                contract_rows,
                preferred_element_type=jnp.float32,
            )
            for stream in range(2)
        ]
    )
    grad_columns = attend_back(columns, attended, logsum, grad_heads, heads_local)
    column_rows = [grad_columns[:split], grad_columns[split:]]
    column_sums = [
        jnp.sum(column_rows[stream], 0, dtype=jnp.float32).reshape(heads_local, 3, HEAD_DIM)
        for stream in range(2)
    ]
    summed = [
        scatter_rows(
            lax.dot_general(
                column_rows[stream],
                weights[0][stream],
                contract_columns,
                preferred_element_type=jnp.float32,
            ).astype(jnp.bfloat16),
            "tensor",
        )
        for stream in range(2)
    ]
    grad_projection = scatter_weights(
        [
            lax.dot_general(
                joined[stream],
                column_rows[stream],
                contract_rows,
                preferred_element_type=jnp.float32,
            )
            for stream in range(2)
        ]
    )
    tensor_rank = lax.axis_index("tensor")
    width_local = heads_local * HEAD_DIM
    hidden_local = preact[0].shape[1]

    def placed(length, values, offset):
        return lax.dynamic_update_slice_in_dim(
            jnp.zeros((length,), jnp.float32), values, offset, 0
        )

    new_grads, slot_grads, bias_grads = ([], [], [])
    for stream in range(2):
        shift_back = jax.vjp(modulate, states[stream], shifts[stream][0], shifts[stream][1])[1]
        back_rows, back_shift, back_scale = shift_back(summed[stream])
        new_grads.append(grad_middle[stream] + back_rows)
        slot_grad = jnp.concatenate(
            [
                back_shift,
                back_scale,
                gate_attend[stream],
                shift_feed[stream],
                scale_feed[stream],
                gate_feed[stream],
            ]
        )
        slot_grads.append(slot_grad)
        bias_grads.append(
            jnp.concatenate(
                [
                    slot_grad,
                    placed(D, column_sums[stream][:, 0].reshape(-1), tensor_rank * width_local),
                    placed(D, column_sums[stream][:, 2].reshape(-1), tensor_rank * width_local),
                    jnp.sum(grad_attend[stream], 0),
                    placed(FF, hidden_sums[stream], tensor_rank * hidden_local),
                    jnp.sum(grad_branch[stream], 0),
                ]
            )
        )
    weight_grads = (grad_projection, grad_recombine, grad_expansion, grad_contraction)
    return (new_grads, weight_grads, jnp.stack(bias_grads), jnp.stack(slot_grads))


def slot_table(silu_rows, modulation, slots):
    size = lax.axis_size("tensor")
    rank = lax.axis_index("tensor")
    count = silu_rows.shape[0]
    partial = jnp.einsum(
        "nd,lsdm->nlsm", silu_rows, modulation.astype(jnp.float32), precision=highest
    ).reshape(count, -1)
    width = partial.shape[1] // size
    owned = 0.0
    for step in range(size):
        block = lax.dynamic_slice_in_dim(partial, (rank ^ step) * width, width, 1)
        owned = owned + (exchange(block, "tensor", step) if step else block)
    onehot = (slots[:, None] == jnp.arange(count, dtype=jnp.int32)[None, :]).astype(jnp.float32)
    per_slot = jnp.dot(onehot, owned, precision=highest)
    mine = per_slot[0]
    for step in range(1, per_slot.shape[0]):
        mine = mine + exchange(per_slot[step], "dp", step)
    table = jnp.zeros((partial.shape[1],), jnp.float32)
    for step, block in enumerate(gather_parts(mine, "tensor")):
        table = lax.dynamic_update_slice_in_dim(table, block, (rank ^ step) * width, 0)
    return table.reshape(LAYERS, 2, -1)


def on_device(
    image_tokens,
    text_tokens,
    conditioning,
    slot_sequence,
    rank_counts,
    projection,
    recombine,
    expansion,
    contraction,
    modulation,
    biases,
    cotangent_image,
    cotangent_text,
):
    tensor_rank = lax.axis_index("tensor")
    flat_rank = lax.axis_index(("dp", "tensor"))
    heads_local = HEADS // lax.axis_size("tensor")
    width_local = heads_local * HEAD_DIM
    hidden_local = FF // lax.axis_size("tensor")
    bias_all = lax.all_gather(biases, ("dp", "tensor"), axis=2, tiled=True).astype(jnp.float32)
    shard_rows = modulation.shape[2]
    owned_rows = lax.dynamic_slice_in_dim(
        jax.nn.silu(conditioning), flat_rank * shard_rows, shard_rows, 1
    )
    slots = jnp.concatenate(gather_parts(slot_sequence, "dp"))
    slot_shifts = slot_table(owned_rows, modulation, slots) + bias_all[:, :, : 6 * D]
    live = (rank_counts[0] > 0).astype(jnp.float32)
    states = [image_tokens.astype(jnp.float32), text_tokens.astype(jnp.float32)]
    stored = []
    for tier in range(LAYERS):
        weights = [
            [
                lax.all_gather(matrix[tier, stream], "dp", axis=0, tiled=True)
                for stream in range(2)
            ]
            for matrix in (projection, recombine, expansion, contraction)
        ]
        pieces = layer_biases(bias_all[tier], tensor_rank, width_local, hidden_local)
        shifts = [
            [slot_shifts[tier, stream, part * D : (part + 1) * D] for part in range(6)]
            for stream in range(2)
        ]
        record, states = forward_layer(states, weights, pieces, shifts, heads_local)
        stored.append((weights, shifts, record))
    gradients = [
        cotangent_image.astype(jnp.float32) * live,
        cotangent_text.astype(jnp.float32) * live,
    ]
    slot_rows = jnp.dot(
        (
            slots[:, None] == jnp.arange(conditioning.shape[0], dtype=jnp.int32)[None, :]
        ).astype(jnp.float32),
        owned_rows,
        precision=highest,
    )
    weight_store, bias_store, modulation_store = ([], [], [])
    for tier in reversed(range(LAYERS)):
        weights, shifts, record = stored[tier]
        gradients, layer_grads, bias_part, slot_grads = backward_layer(
            gradients, record, weights, shifts, heads_local
        )
        weight_store.insert(0, layer_grads)
        bias_store.insert(0, bias_part)
        slot_sums = jnp.stack(gather_parts(sum_over(slot_grads, "tensor"), "dp"))
        modulation_store.insert(
            0, jnp.einsum("pd,psm->sdm", slot_rows, slot_sums, precision=highest)
        )
    stacked = [
        jnp.stack([jnp.stack(entry[kind]) for entry in weight_store]) for kind in range(4)
    ]
    biases_grad = lax.psum_scatter(
        jnp.stack(bias_store), ("dp", "tensor"), scatter_dimension=2, tiled=True
    )
    return (
        (states[0] * live).astype(jnp.bfloat16),
        (states[1] * live).astype(jnp.bfloat16),
        gradients[0],
        gradients[1],
        stacked[0],
        stacked[1],
        stacked[2],
        stacked[3],
        jnp.stack(modulation_store),
        biases_grad,
    )


def solution(mesh):
    in_specs = (
        P(("dp", "tensor"), None),
        P(("dp", "tensor"), None),
        P(),
        P("dp"),
        P("dp"),
        P(None, None, "dp", "tensor"),
        P(None, None, "dp", "tensor"),
        P(None, None, "dp", "tensor"),
        P(None, None, "dp", "tensor"),
        P(None, None, ("dp", "tensor"), None),
        P(None, None, ("dp", "tensor")),
        P(("dp", "tensor"), None),
        P(("dp", "tensor"), None),
    )
    out_specs = (
        P(("dp", "tensor"), None),
        P(("dp", "tensor"), None),
        P(("dp", "tensor"), None),
        P(("dp", "tensor"), None),
        P(None, None, "dp", "tensor"),
        P(None, None, "dp", "tensor"),
        P(None, None, "dp", "tensor"),
        P(None, None, "dp", "tensor"),
        P(None, None, ("dp", "tensor"), None),
        P(None, None, ("dp", "tensor")),
    )
    return jax.shard_map(
        on_device, mesh=mesh, in_specs=in_specs, out_specs=out_specs, check_vma=False
    )
```

```python
import functools
import math

import jax
import jax.numpy as jnp
from jax import lax
from jax.experimental import pallas as pl
from jax.experimental.pallas import tpu as pltpu
from jax.sharding import PartitionSpec as P

D = 1536
HEADS = 24
HEAD_DIM = 64
FF = 6144
LAYERS = 2

highest = lax.Precision.HIGHEST
contract_columns = (((1,), (1,)), ((), ()))
contract_rows = (((0,), (0,)), ((), ()))
SCALE = HEAD_DIM ** (-0.5)
EXPONENT = SCALE * math.log2(math.e)


def normalize(values):
    average = jnp.mean(values, -1, keepdims=True)
    centred = values - average
    spread = jnp.mean(centred * centred, -1, keepdims=True)
    return centred * lax.rsqrt(spread + 1e-06)


def modulate(values, shifts, scales):
    return normalize(values) * (1.0 + scales) + shifts


def gelu_tanh(values):
    return jax.nn.gelu(values, approximate=True)


def exchange(values, axis, step):
    size = lax.axis_size(axis)
    return lax.ppermute(values, axis, [(rank, rank ^ step) for rank in range(size)])


def gather_parts(values, axis):
    return [values] + [exchange(values, axis, step) for step in range(1, lax.axis_size(axis))]


def gather_rows(values, axis):
    return jnp.concatenate(gather_parts(values, axis), axis=0)


def scatter_rows(values, axis):
    size = lax.axis_size(axis)
    rows = values.shape[0] // size
    total = values[:rows].astype(jnp.float32)
    for step in range(1, size):
        total = total + exchange(values[step * rows : (step + 1) * rows], axis, step).astype(
            jnp.float32
        )
    return total


def sum_over(values, axis):
    total = values
    for step in range(1, lax.axis_size(axis)):
        total = total + exchange(values, axis, step)
    return total


def after(values, *needed):
    return lax.optimization_barrier((values, needed))[0]


def spread_kernel(chunks_ref, out_ref):
    count, _, width = chunks_ref.shape
    for place in range(count):
        out_ref[:, place * width : (place + 1) * width] = chunks_ref[place]


def split_kernel(values_ref, out_ref):
    count, _, width = out_ref.shape
    for place in range(count):
        out_ref[place] = values_ref[:, place * width : (place + 1) * width]


def gather_biases(biases):
    width = biases.shape[2]
    held = biases.reshape(1, LAYERS * 2, width)
    held = gather_rows(gather_rows(held, "tensor")[None], "dp")
    outer, inner = held.shape[:2]
    chunks = held.reshape(outer * inner, -1).astype(jnp.float32)
    order = (
        (jnp.arange(outer, dtype=jnp.int32) ^ lax.axis_index("dp"))[:, None] * inner
        + (jnp.arange(inner, dtype=jnp.int32) ^ lax.axis_index("tensor"))[None, :]
    ).reshape(-1)
    select = (
        order[:, None] == jnp.arange(outer * inner, dtype=jnp.int32)[None, :]
    ).astype(jnp.float32)
    ordered = jnp.dot(select, chunks, precision=highest)
    spread = pl.pallas_call(
        spread_kernel,
        out_shape=jax.ShapeDtypeStruct((LAYERS * 2, outer * inner * width), jnp.float32),
        name="spread",
    )(ordered.reshape(outer * inner, LAYERS * 2, width))
    return spread.reshape(LAYERS, 2, -1)


def scatter_biases(values, width):
    outer, inner = lax.axis_size("dp"), lax.axis_size("tensor")
    chunks = pl.pallas_call(
        split_kernel,
        out_shape=jax.ShapeDtypeStruct((outer * inner, LAYERS * 2, width), jnp.float32),
        name="split",
    )(values.reshape(LAYERS * 2, -1))
    chunks = chunks.reshape(outer, inner, LAYERS * 2, width)
    for axis, size in (("dp", outer), ("tensor", inner)):
        rank = lax.axis_index(axis)
        total = lax.dynamic_index_in_dim(chunks, rank, 0, False)
        for step in range(1, size):
            block = lax.dynamic_index_in_dim(chunks, rank ^ step, 0, False)
            total = total + exchange(block, axis, step)
        chunks = total
    return chunks.reshape(LAYERS, 2, width)


def row_block(rows):
    for block in (384, 256, 128):
        if rows % block == 0:
            return block
    return rows


def attend_kernel(heads, block, columns_ref, out_ref, log_ref):
    rows = columns_ref.shape[0]
    for head in range(heads):
        base = head * 3 * HEAD_DIM
        keys = columns_ref[:, base + HEAD_DIM : base + 2 * HEAD_DIM]
        values = columns_ref[:, base + 2 * HEAD_DIM : base + 3 * HEAD_DIM]

        def step(index, carry):
            place = pl.ds(pl.multiple_of(index * block, block), block)
            queries = columns_ref[place, base : base + HEAD_DIM]
            scores = lax.dot_general(
                queries, keys, contract_columns, preferred_element_type=jnp.float32
            )
            row_max = jnp.max(scores, -1, keepdims=True)
            weights = jnp.exp2((scores - row_max) * EXPONENT)
            totals = jnp.sum(weights, -1, keepdims=True)
            output = jnp.dot(
                weights.astype(jnp.bfloat16), values, preferred_element_type=jnp.float32
            )
            out_ref[place, head * HEAD_DIM : (head + 1) * HEAD_DIM] = (output / totals).astype(
                jnp.bfloat16
            )
            log_ref[place, head : head + 1] = row_max * EXPONENT + jnp.log2(totals)
            return carry

        lax.fori_loop(0, rows // block, step, 0)


def attend(columns, heads):
    rows = columns.shape[0]
    return pl.pallas_call(
        functools.partial(attend_kernel, heads, row_block(rows)),
        out_shape=(
            jax.ShapeDtypeStruct((rows, heads * HEAD_DIM), jnp.bfloat16),
            jax.ShapeDtypeStruct((rows, 128), jnp.float32),
        ),
        cost_estimate=pl.CostEstimate(
            flops=heads * rows * rows * HEAD_DIM * 4,
            bytes_accessed=columns.size * 3,
            transcendentals=heads * rows * rows,
        ),
        name="attend",
    )(columns)


def attend_back_kernel(
    heads, block, columns_ref, out_ref, log_ref, grad_ref, result_ref, key_acc, value_acc
):
    rows = columns_ref.shape[0]
    for head in range(heads):
        base = head * 3 * HEAD_DIM
        part = slice(head * HEAD_DIM, (head + 1) * HEAD_DIM)
        keys = columns_ref[:, base + HEAD_DIM : base + 2 * HEAD_DIM]
        values = columns_ref[:, base + 2 * HEAD_DIM : base + 3 * HEAD_DIM]
        key_acc[...] = jnp.zeros_like(key_acc)
        value_acc[...] = jnp.zeros_like(value_acc)

        def step(index, carry):
            place = pl.ds(pl.multiple_of(index * block, block), block)
            queries = columns_ref[place, base : base + HEAD_DIM]
            grad_out = grad_ref[place, part]
            inner = jnp.sum(
                grad_out.astype(jnp.float32) * out_ref[place, part].astype(jnp.float32),
                -1,
                keepdims=True,
            )
            scores = lax.dot_general(
                queries, keys, contract_columns, preferred_element_type=jnp.float32
            )
            weights = jnp.exp2(scores * EXPONENT - log_ref[place, head : head + 1])
            grad_weights = lax.dot_general(
                grad_out, values, contract_columns, preferred_element_type=jnp.float32
            )
            grad_scores = (weights * (grad_weights - inner)).astype(jnp.bfloat16)
            result_ref[place, base : base + HEAD_DIM] = (
                jnp.dot(grad_scores, keys, preferred_element_type=jnp.float32) * SCALE
            ).astype(jnp.bfloat16)
            key_acc[...] += lax.dot_general(
                grad_scores, queries, contract_rows, preferred_element_type=jnp.float32
            )
            value_acc[...] += lax.dot_general(
                weights.astype(jnp.bfloat16),
                grad_out,
                contract_rows,
                preferred_element_type=jnp.float32,
            )
            return carry

        lax.fori_loop(0, rows // block, step, 0)
        result_ref[:, base + HEAD_DIM : base + 2 * HEAD_DIM] = (key_acc[...] * SCALE).astype(
            jnp.bfloat16
        )
        result_ref[:, base + 2 * HEAD_DIM : base + 3 * HEAD_DIM] = value_acc[...].astype(
            jnp.bfloat16
        )


def attend_back(columns, output, logsum, grad_output, heads):
    rows = columns.shape[0]
    return pl.pallas_call(
        functools.partial(attend_back_kernel, heads, row_block(rows)),
        out_shape=jax.ShapeDtypeStruct(columns.shape, jnp.bfloat16),
        scratch_shapes=[
            pltpu.VMEM((rows, HEAD_DIM), jnp.float32),
            pltpu.VMEM((rows, HEAD_DIM), jnp.float32),
        ],
        cost_estimate=pl.CostEstimate(
            flops=heads * rows * rows * HEAD_DIM * 10,
            bytes_accessed=columns.size * 6,
            transcendentals=heads * rows * rows,
        ),
        name="attend_back",
    )(columns, output, logsum, grad_output)


def column_bias(query_bias, value_bias, heads):
    query_part = query_bias.reshape(heads, HEAD_DIM)
    value_part = value_bias.reshape(heads, HEAD_DIM)
    return jnp.stack([query_part, jnp.zeros_like(query_part), value_part], axis=1).reshape(-1)


def layer_biases(bias_layer, tensor_rank, width_local, hidden_local):
    query_bias = lax.dynamic_slice_in_dim(
        bias_layer, 6 * D + tensor_rank * width_local, width_local, 1
    )
    value_bias = lax.dynamic_slice_in_dim(
        bias_layer, 7 * D + tensor_rank * width_local, width_local, 1
    )
    out_bias = bias_layer[:, 8 * D : 9 * D]
    hidden_bias = lax.dynamic_slice_in_dim(
        bias_layer, 9 * D + tensor_rank * hidden_local, hidden_local, 1
    )
    last_bias = bias_layer[:, 9 * D + FF :]
    return (query_bias, value_bias, out_bias, hidden_bias, last_bias)


def forward_layer(states, weights, pieces, shifts, heads_local):
    query_bias, value_bias, out_bias, hidden_bias, last_bias = pieces
    joined = [
        gather_rows(
            modulate(states[stream], shifts[stream][0], shifts[stream][1]).astype(jnp.bfloat16),
            "tensor",
        )
        for stream in range(2)
    ]
    columns = jnp.concatenate(
        [
            (
                jnp.dot(joined[stream], weights[0][stream], preferred_element_type=jnp.float32)
                + column_bias(query_bias[stream], value_bias[stream], heads_local)
            ).astype(jnp.bfloat16)
            for stream in range(2)
        ]
    )
    attended, logsum = attend(columns, heads_local)
    split = joined[0].shape[0]
    out_rows = [attended[:split], attended[split:]]
    branch_attend = [
        scatter_rows(
            lax.dot_general(
                out_rows[stream],
                weights[1][stream],
                contract_columns,
                preferred_element_type=jnp.float32,
            ).astype(jnp.bfloat16),
            "tensor",
        )
        + out_bias[stream]
        for stream in range(2)
    ]
    middle = [states[stream] + shifts[stream][2] * branch_attend[stream] for stream in range(2)]
    joined_feed = [
        gather_rows(
            modulate(middle[stream], shifts[stream][3], shifts[stream][4]).astype(jnp.bfloat16),
            "tensor",
        )
        for stream in range(2)
    ]
    preact = [
        jnp.dot(joined_feed[stream], weights[2][stream], preferred_element_type=jnp.float32)
        + hidden_bias[stream]
        for stream in range(2)
    ]
    activated = [gelu_tanh(preact[stream]).astype(jnp.bfloat16) for stream in range(2)]
    branch_feed = [
        scatter_rows(
            lax.dot_general(
                activated[stream],
                weights[3][stream],
                contract_columns,
                preferred_element_type=jnp.float32,
            ).astype(jnp.bfloat16),
            "tensor",
        )
        + last_bias[stream]
        for stream in range(2)
    ]
    result = [middle[stream] + shifts[stream][5] * branch_feed[stream] for stream in range(2)]
    record = (
        states,
        joined,
        columns,
        attended,
        logsum,
        branch_attend,
        middle,
        joined_feed,
        preact,
        activated,
        branch_feed,
    )
    return (record, result)


def weight_grads_kernel(count, *refs):
    out_ref = refs[-1]
    offset = 0
    for index in range(count):
        left, right = refs[2 * index], refs[2 * index + 1]
        width = right.shape[1]
        tile = 384 if width % 384 == 0 else width
        for place in range(0, width, tile):
            out_ref[:, offset + place : offset + place + tile] = lax.dot_general(
                left[...],
                right[:, place : place + tile],
                contract_rows,
                preferred_element_type=jnp.float32,
            ).astype(jnp.bfloat16)
        offset += width


def weight_grads(pairs):
    tile = 256
    specs, operands, total, flops, moved = ([], [], 0, 0, 0)
    for left, right, place in pairs:
        rows, width = left.shape[0], right.shape[1]
        specs.append(pl.BlockSpec((rows, tile), lambda index: (0, index)))
        specs.append(pl.BlockSpec((rows, width), lambda index, place=place: (place, 0)))
        operands += [left, right]
        total += width
        flops += 2 * rows * width * left.shape[1]
        moved += 2 * (left.size + rows * width)
    depth = pairs[0][0].shape[1]
    return pl.pallas_call(
        functools.partial(weight_grads_kernel, len(pairs)),
        grid=(depth // tile,),
        in_specs=specs,
        out_specs=pl.BlockSpec((tile, total), lambda index: (index, 0)),
        out_shape=jax.ShapeDtypeStruct((depth, total), jnp.bfloat16),
        cost_estimate=pl.CostEstimate(
            flops=flops, bytes_accessed=moved + 2 * depth * total, transcendentals=0
        ),
        name="weight_grads",
    )(*operands)


def scatter_weights(grads):
    return lax.psum_scatter(grads, "dp", scatter_dimension=0, tiled=True)


def unpack_weights(shares, offset, width):
    return jnp.stack(
        [
            shares[:, offset + stream * width : offset + (stream + 1) * width].astype(jnp.float32)
            for stream in range(2)
        ]
    )


def backward_layer(gradients, record, weights, shifts, heads_local, pending):
    (
        states,
        joined,
        columns,
        attended,
        logsum,
        branch_attend,
        middle,
        joined_feed,
        preact,
        activated,
        branch_feed,
    ) = record
    split = joined[0].shape[0]
    out_rows = [attended[:split], attended[split:]]
    grad_branch = [shifts[stream][5] * gradients[stream] for stream in range(2)]
    gate_feed = [jnp.sum(gradients[stream] * branch_feed[stream], 0) for stream in range(2)]
    branch_rows = [
        gather_rows(grad_branch[stream].astype(jnp.bfloat16), "tensor") for stream in range(2)
    ]
    grad_contraction = weight_grads(
        [(branch_rows[stream], activated[stream], 0) for stream in range(2)]
    )
    branch_rows, feed_weights = after((branch_rows, weights[3]), grad_contraction, *pending[:1])
    grad_contraction = scatter_weights(grad_contraction)
    grad_preact = []
    for stream in range(2):
        grad_activated = jnp.dot(
            branch_rows[stream], feed_weights[stream], preferred_element_type=jnp.float32
        )
        gelu_back = jax.vjp(gelu_tanh, preact[stream])[1]
        grad_preact.append(gelu_back(grad_activated)[0].astype(jnp.bfloat16))
    hidden_sums = [jnp.sum(grad_preact[stream], 0, dtype=jnp.float32) for stream in range(2)]
    summed = [
        scatter_rows(
            lax.dot_general(
                grad_preact[stream],
                weights[2][stream],
                contract_columns,
                preferred_element_type=jnp.float32,
            ).astype(jnp.bfloat16),
            "tensor",
        )
        for stream in range(2)
    ]
    grad_expansion = weight_grads(
        [(joined_feed[stream], grad_preact[stream], 0) for stream in range(2)]
    )
    summed = after(summed, grad_expansion)
    grad_expansion = scatter_weights(grad_expansion)
    grad_middle, shift_feed, scale_feed = ([], [], [])
    summed = after(summed, *pending[1:])
    for stream in range(2):
        shift_back = jax.vjp(modulate, middle[stream], shifts[stream][3], shifts[stream][4])[1]
        back_rows, back_shift, back_scale = shift_back(summed[stream])
        grad_middle.append(gradients[stream] + back_rows)
        shift_feed.append(back_shift)
        scale_feed.append(back_scale)
    grad_attend = [shifts[stream][2] * grad_middle[stream] for stream in range(2)]
    gate_attend = [jnp.sum(grad_middle[stream] * branch_attend[stream], 0) for stream in range(2)]
    attend_rows = [
        gather_rows(grad_attend[stream].astype(jnp.bfloat16), "tensor") for stream in range(2)
    ]
    grad_heads = jnp.concatenate(
        [
            jnp.dot(
                attend_rows[stream], weights[1][stream], preferred_element_type=jnp.float32
            ).astype(jnp.bfloat16)
            for stream in range(2)
        ]
    )
    grad_columns = attend_back(columns, attended, logsum, grad_heads, heads_local)
    column_rows = [grad_columns[:split], grad_columns[split:]]
    column_sums = [
        jnp.sum(column_rows[stream], 0, dtype=jnp.float32).reshape(heads_local, 3, HEAD_DIM)
        for stream in range(2)
    ]
    summed = [
        scatter_rows(
            lax.dot_general(
                column_rows[stream],
                weights[0][stream],
                contract_columns,
                preferred_element_type=jnp.float32,
            ).astype(jnp.bfloat16),
            "tensor",
        )
        for stream in range(2)
    ]
    text_place = split // attend_rows[1].shape[0]
    grad_attention = weight_grads(
        [
            (attend_rows[0], attended, 0),
            (attend_rows[1], attended, text_place),
            (joined[0], grad_columns, 0),
            (joined[1], grad_columns, text_place),
        ]
    )
    summed = after(summed, grad_attention)
    grad_attention = scatter_weights(grad_attention)
    tensor_rank = lax.axis_index("tensor")
    width_local = heads_local * HEAD_DIM
    hidden_local = preact[0].shape[1]

    def placed(length, values, offset):
        return lax.dynamic_update_slice_in_dim(
            jnp.zeros((length,), jnp.float32), values, offset, 0
        )

    new_grads, slot_grads, bias_grads = ([], [], [])
    for stream in range(2):
        shift_back = jax.vjp(modulate, states[stream], shifts[stream][0], shifts[stream][1])[1]
        back_rows, back_shift, back_scale = shift_back(summed[stream])
        new_grads.append(grad_middle[stream] + back_rows)
        slot_grad = jnp.concatenate(
            [
                back_shift,
                back_scale,
                gate_attend[stream],
                shift_feed[stream],
                scale_feed[stream],
                gate_feed[stream],
            ]
        )
        slot_grads.append(slot_grad)
        bias_grads.append(
            jnp.concatenate(
                [
                    slot_grad,
                    placed(D, column_sums[stream][:, 0].reshape(-1), tensor_rank * width_local),
                    placed(D, column_sums[stream][:, 2].reshape(-1), tensor_rank * width_local),
                    jnp.sum(grad_attend[stream], 0),
                    placed(FF, hidden_sums[stream], tensor_rank * hidden_local),
                    jnp.sum(grad_branch[stream], 0),
                ]
            )
        )
    out_width = attended.shape[1]
    layer_grads = (
        unpack_weights(grad_attention, 2 * out_width, 3 * out_width),
        unpack_weights(grad_attention, 0, out_width),
        unpack_weights(grad_expansion, 0, hidden_local),
        unpack_weights(grad_contraction, 0, hidden_local),
    )
    pending = (grad_contraction, grad_expansion, grad_attention)
    return (new_grads, layer_grads, pending, jnp.stack(bias_grads), jnp.stack(slot_grads))


def slot_table(silu_rows, modulation, slots):
    size = lax.axis_size("tensor")
    rank = lax.axis_index("tensor")
    count = silu_rows.shape[0]
    partial = jnp.einsum(
        "nd,lsdm->nlsm", silu_rows, modulation.astype(jnp.float32), precision=highest
    ).reshape(count, -1)
    width = partial.shape[1] // size
    owned = 0.0
    for step in range(size):
        block = lax.dynamic_slice_in_dim(partial, (rank ^ step) * width, width, 1)
        owned = owned + (exchange(block, "tensor", step) if step else block)
    onehot = (slots[:, None] == jnp.arange(count, dtype=jnp.int32)[None, :]).astype(jnp.float32)
    per_slot = jnp.dot(onehot, owned, precision=highest)
    mine = per_slot[0]
    for step in range(1, per_slot.shape[0]):
        mine = mine + exchange(per_slot[step], "dp", step)
    table = jnp.zeros((partial.shape[1],), jnp.float32)
    for step, block in enumerate(gather_parts(mine, "tensor")):
        table = lax.dynamic_update_slice_in_dim(table, block, (rank ^ step) * width, 0)
    return table.reshape(LAYERS, 2, -1)


def on_device(
    image_tokens,
    text_tokens,
    conditioning,
    slot_sequence,
    rank_counts,
    projection,
    recombine,
    expansion,
    contraction,
    modulation,
    biases,
    cotangent_image,
    cotangent_text,
):
    tensor_rank = lax.axis_index("tensor")
    flat_rank = lax.axis_index(("dp", "tensor"))
    heads_local = HEADS // lax.axis_size("tensor")
    width_local = heads_local * HEAD_DIM
    hidden_local = FF // lax.axis_size("tensor")
    bias_all = gather_biases(biases)
    shard_rows = modulation.shape[2]
    owned_rows = lax.dynamic_slice_in_dim(
        jax.nn.silu(conditioning), flat_rank * shard_rows, shard_rows, 1
    )
    slots = jnp.concatenate(gather_parts(slot_sequence, "dp"))
    slot_shifts = slot_table(owned_rows, modulation, slots) + bias_all[:, :, : 6 * D]
    live = (rank_counts[0] > 0).astype(jnp.float32)
    states = [image_tokens.astype(jnp.float32), text_tokens.astype(jnp.float32)]
    stored = []
    for tier in range(LAYERS):
        weights = [
            lax.all_gather(matrix[tier], "dp", axis=1, tiled=True)
            for matrix in (projection, recombine, expansion, contraction)
        ]
        pieces = layer_biases(bias_all[tier], tensor_rank, width_local, hidden_local)
        shifts = [
            [slot_shifts[tier, stream, part * D : (part + 1) * D] for part in range(6)]
            for stream in range(2)
        ]
        record, states = forward_layer(states, weights, pieces, shifts, heads_local)
        stored.append((weights, shifts, record))
    gradients = [
        cotangent_image.astype(jnp.float32) * live,
        cotangent_text.astype(jnp.float32) * live,
    ]
    slot_rows = jnp.dot(
        (
            slots[:, None] == jnp.arange(conditioning.shape[0], dtype=jnp.int32)[None, :]
        ).astype(jnp.float32),
        owned_rows,
        precision=highest,
    )
    weight_store, bias_store, modulation_store, pending = ([], [], [], ())
    for tier in reversed(range(LAYERS)):
        weights, shifts, record = stored[tier]
        gradients, layer_grads, pending, bias_part, slot_grads = backward_layer(
            gradients, record, weights, shifts, heads_local, pending
        )
        weight_store.insert(0, layer_grads)
        bias_store.insert(0, bias_part)
        slot_sums = jnp.stack(gather_parts(sum_over(slot_grads, "tensor"), "dp"))
        modulation_store.insert(
            0, jnp.einsum("pd,psm->sdm", slot_rows, slot_sums, precision=highest)
        )
    stacked = [
        jnp.stack([entry[kind] for entry in weight_store]) for kind in range(4)
    ]
    biases_grad = scatter_biases(jnp.stack(bias_store), biases.shape[2])
    return (
        (states[0] * live).astype(jnp.bfloat16),
        (states[1] * live).astype(jnp.bfloat16),
        gradients[0],
        gradients[1],
        stacked[0],
        stacked[1],
        stacked[2],
        stacked[3],
        jnp.stack(modulation_store),
        biases_grad,
    )


def solution(mesh):
    in_specs = (
        P(("dp", "tensor"), None),
        P(("dp", "tensor"), None),
        P(),
        P("dp"),
        P("dp"),
        P(None, None, "dp", "tensor"),
        P(None, None, "dp", "tensor"),
        P(None, None, "dp", "tensor"),
        P(None, None, "dp", "tensor"),
        P(None, None, ("dp", "tensor"), None),
        P(None, None, ("dp", "tensor")),
        P(("dp", "tensor"), None),
        P(("dp", "tensor"), None),
    )
    out_specs = (
        P(("dp", "tensor"), None),
        P(("dp", "tensor"), None),
        P(("dp", "tensor"), None),
        P(("dp", "tensor"), None),
        P(None, None, "dp", "tensor"),
        P(None, None, "dp", "tensor"),
        P(None, None, "dp", "tensor"),
        P(None, None, "dp", "tensor"),
        P(None, None, ("dp", "tensor"), None),
        P(None, None, ("dp", "tensor")),
    )
    return jax.shard_map(
        on_device, mesh=mesh, in_specs=in_specs, out_specs=out_specs, check_vma=False
    )
```

```python
import functools
import math

import jax
import jax.numpy as jnp
from jax import lax
from jax.experimental import pallas as pl
from jax.experimental.pallas import tpu as pltpu
from jax.sharding import PartitionSpec as P

D = 1536
HEADS = 24
HEAD_DIM = 64
FF = 6144
LAYERS = 2

highest = lax.Precision.HIGHEST
contract_columns = (((1,), (1,)), ((), ()))
contract_rows = (((0,), (0,)), ((), ()))
SCALE = HEAD_DIM ** (-0.5)
EXPONENT = SCALE * math.log2(math.e)


def normalize(values):
    average = jnp.mean(values, -1, keepdims=True)
    centred = values - average
    spread = jnp.mean(centred * centred, -1, keepdims=True)
    return centred * lax.rsqrt(spread + 1e-06)


def modulate(values, shifts, scales):
    return normalize(values) * (1.0 + scales) + shifts


def gelu_tanh(values):
    return jax.nn.gelu(values, approximate=True)


def exchange(values, axis, step):
    size = lax.axis_size(axis)
    return lax.ppermute(values, axis, [(rank, rank ^ step) for rank in range(size)])


def gather_parts(values, axis):
    return [values] + [exchange(values, axis, step) for step in range(1, lax.axis_size(axis))]


def gather_rows(values, axis):
    return jnp.concatenate(gather_parts(values, axis), axis=0)


def gather_streams(streams):
    counts = [values.shape[0] for values in streams]
    rows = jnp.concatenate(streams)
    if lax.axis_size("tensor") == 4:
        half = rows.shape[0] // 2
        first, second = (exchange(rows, "tensor", step) for step in (1, 2))
        far = jnp.concatenate(
            [exchange(first[:half], "tensor", 2), exchange(second[half:], "tensor", 1)]
        )
        parts = [rows, first, second, far]
    else:
        parts = gather_parts(rows, "tensor")
    return [
        jnp.concatenate([part[: counts[0]] for part in parts]),
        jnp.concatenate([part[counts[0] :] for part in parts]),
    ]


def scatter_streams(left, right):
    size = lax.axis_size("tensor")
    counts = [values.shape[0] // size for values in left]

    def piece(step):
        return jnp.concatenate(
            [
                lax.dot_general(
                    left[stream][step * counts[stream] : (step + 1) * counts[stream]],
                    right[stream],
                    contract_columns,
                    preferred_element_type=jnp.float32,
                ).astype(jnp.bfloat16)
                for stream in range(2)
            ]
        )

    if size == 4:
        half = sum(counts) // 2
        far = lax.optimization_barrier(piece(3))
        first_in = exchange(far[:half], "tensor", 1)
        second_in = exchange(far[half:], "tensor", 2)
        first, second = lax.optimization_barrier((piece(1), piece(2)))
        first = jnp.concatenate([first[:half], first[half:] + second_in])
        second = jnp.concatenate([second[:half] + first_in, second[half:]])
        pieces = [exchange(first, "tensor", 1), exchange(second, "tensor", 2)]
    else:
        far = piece(size - 1)
        pieces = [exchange(far, "tensor", size - 1)]
        pieces += [exchange(piece(step), "tensor", step) for step in range(1, size - 1)]
    total = piece(0).astype(jnp.float32)
    for values in pieces:
        total = total + values.astype(jnp.float32)
    return [total[: counts[0]], total[counts[0] :]], far


def sum_over(values, axis):
    total = values
    for step in range(1, lax.axis_size(axis)):
        total = total + exchange(values, axis, step)
    return total


def after(values, *needed):
    return lax.optimization_barrier((values, needed))[0]


def spread_kernel(chunks_ref, out_ref):
    count, _, width = chunks_ref.shape
    for place in range(count):
        out_ref[:, place * width : (place + 1) * width] = chunks_ref[place]


def split_kernel(values_ref, out_ref):
    count, _, width = out_ref.shape
    for place in range(count):
        out_ref[place] = values_ref[:, place * width : (place + 1) * width]


def gather_biases(biases):
    width = biases.shape[2]
    held = biases.reshape(1, LAYERS * 2, width)
    held = gather_rows(gather_rows(held, "tensor")[None], "dp")
    outer, inner = held.shape[:2]
    chunks = held.reshape(outer * inner, -1).astype(jnp.float32)
    order = (
        (jnp.arange(outer, dtype=jnp.int32) ^ lax.axis_index("dp"))[:, None] * inner
        + (jnp.arange(inner, dtype=jnp.int32) ^ lax.axis_index("tensor"))[None, :]
    ).reshape(-1)
    select = (
        order[:, None] == jnp.arange(outer * inner, dtype=jnp.int32)[None, :]
    ).astype(jnp.float32)
    ordered = jnp.dot(select, chunks, precision=highest)
    spread = pl.pallas_call(
        spread_kernel,
        out_shape=jax.ShapeDtypeStruct((LAYERS * 2, outer * inner * width), jnp.float32),
        name="spread",
    )(ordered.reshape(outer * inner, LAYERS * 2, width))
    return spread.reshape(LAYERS, 2, -1)


def scatter_biases(values, width):
    outer, inner = lax.axis_size("dp"), lax.axis_size("tensor")
    chunks = pl.pallas_call(
        split_kernel,
        out_shape=jax.ShapeDtypeStruct((outer * inner, LAYERS * 2, width), jnp.float32),
        name="split",
    )(values.reshape(LAYERS * 2, -1))
    chunks = chunks.reshape(outer, inner, LAYERS * 2, width)
    for axis, size in (("dp", outer), ("tensor", inner)):
        rank = lax.axis_index(axis)
        total = lax.dynamic_index_in_dim(chunks, rank, 0, False)
        for step in range(1, size):
            block = lax.dynamic_index_in_dim(chunks, rank ^ step, 0, False)
            total = total + exchange(block, axis, step)
        chunks = total
    return chunks.reshape(LAYERS, 2, width)


def row_block(rows):
    for block in (384, 256, 128):
        if rows % block == 0:
            return block
    return rows


def attend_kernel(heads, block, columns_ref, out_ref, log_ref):
    rows = columns_ref.shape[0]
    for head in range(heads):
        base = head * 3 * HEAD_DIM
        keys = columns_ref[:, base + HEAD_DIM : base + 2 * HEAD_DIM]
        values = columns_ref[:, base + 2 * HEAD_DIM : base + 3 * HEAD_DIM]

        def step(index, carry):
            place = pl.ds(pl.multiple_of(index * block, block), block)
            queries = columns_ref[place, base : base + HEAD_DIM]
            scores = lax.dot_general(
                queries, keys, contract_columns, preferred_element_type=jnp.float32
            )
            row_max = jnp.max(scores, -1, keepdims=True)
            weights = jnp.exp2((scores - row_max) * EXPONENT)
            totals = jnp.sum(weights, -1, keepdims=True)
            output = jnp.dot(
                weights.astype(jnp.bfloat16), values, preferred_element_type=jnp.float32
            )
            out_ref[place, head * HEAD_DIM : (head + 1) * HEAD_DIM] = (output / totals).astype(
                jnp.bfloat16
            )
            log_ref[place, head : head + 1] = row_max * EXPONENT + jnp.log2(totals)
            return carry

        lax.fori_loop(0, rows // block, step, 0)


def attend(columns, heads):
    rows = columns.shape[0]
    return pl.pallas_call(
        functools.partial(attend_kernel, heads, row_block(rows)),
        out_shape=(
            jax.ShapeDtypeStruct((rows, heads * HEAD_DIM), jnp.bfloat16),
            jax.ShapeDtypeStruct((rows, 128), jnp.float32),
        ),
        cost_estimate=pl.CostEstimate(
            flops=heads * rows * rows * HEAD_DIM * 4,
            bytes_accessed=columns.size * 3,
            transcendentals=heads * rows * rows,
        ),
        name="attend",
    )(columns)


def attend_back_kernel(
    heads, block, columns_ref, out_ref, log_ref, grad_ref, result_ref, key_acc, value_acc
):
    rows = columns_ref.shape[0]
    for head in range(heads):
        base = head * 3 * HEAD_DIM
        part = slice(head * HEAD_DIM, (head + 1) * HEAD_DIM)
        keys = columns_ref[:, base + HEAD_DIM : base + 2 * HEAD_DIM]
        values = columns_ref[:, base + 2 * HEAD_DIM : base + 3 * HEAD_DIM]
        key_acc[...] = jnp.zeros_like(key_acc)
        value_acc[...] = jnp.zeros_like(value_acc)

        def step(index, carry):
            place = pl.ds(pl.multiple_of(index * block, block), block)
            queries = columns_ref[place, base : base + HEAD_DIM]
            grad_out = grad_ref[place, part]
            inner = jnp.sum(
                grad_out.astype(jnp.float32) * out_ref[place, part].astype(jnp.float32),
                -1,
                keepdims=True,
            )
            scores = lax.dot_general(
                queries, keys, contract_columns, preferred_element_type=jnp.float32
            )
            weights = jnp.exp2(scores * EXPONENT - log_ref[place, head : head + 1])
            grad_weights = lax.dot_general(
                grad_out, values, contract_columns, preferred_element_type=jnp.float32
            )
            grad_scores = (weights * (grad_weights - inner)).astype(jnp.bfloat16)
            result_ref[place, base : base + HEAD_DIM] = (
                jnp.dot(grad_scores, keys, preferred_element_type=jnp.float32) * SCALE
            ).astype(jnp.bfloat16)
            key_acc[...] += lax.dot_general(
                grad_scores, queries, contract_rows, preferred_element_type=jnp.float32
            )
            value_acc[...] += lax.dot_general(
                weights.astype(jnp.bfloat16),
                grad_out,
                contract_rows,
                preferred_element_type=jnp.float32,
            )
            return carry

        lax.fori_loop(0, rows // block, step, 0)
        result_ref[:, base + HEAD_DIM : base + 2 * HEAD_DIM] = (key_acc[...] * SCALE).astype(
            jnp.bfloat16
        )
        result_ref[:, base + 2 * HEAD_DIM : base + 3 * HEAD_DIM] = value_acc[...].astype(
            jnp.bfloat16
        )


def attend_back(columns, output, logsum, grad_output, heads):
    rows = columns.shape[0]
    return pl.pallas_call(
        functools.partial(attend_back_kernel, heads, row_block(rows)),
        out_shape=jax.ShapeDtypeStruct(columns.shape, jnp.bfloat16),
        scratch_shapes=[
            pltpu.VMEM((rows, HEAD_DIM), jnp.float32),
            pltpu.VMEM((rows, HEAD_DIM), jnp.float32),
        ],
        cost_estimate=pl.CostEstimate(
            flops=heads * rows * rows * HEAD_DIM * 10,
            bytes_accessed=columns.size * 6,
            transcendentals=heads * rows * rows,
        ),
        name="attend_back",
    )(columns, output, logsum, grad_output)


def column_bias(query_bias, value_bias, heads):
    query_part = query_bias.reshape(heads, HEAD_DIM)
    value_part = value_bias.reshape(heads, HEAD_DIM)
    return jnp.stack([query_part, jnp.zeros_like(query_part), value_part], axis=1).reshape(-1)


def layer_biases(bias_layer, tensor_rank, width_local, hidden_local):
    query_bias = lax.dynamic_slice_in_dim(
        bias_layer, 6 * D + tensor_rank * width_local, width_local, 1
    )
    value_bias = lax.dynamic_slice_in_dim(
        bias_layer, 7 * D + tensor_rank * width_local, width_local, 1
    )
    out_bias = bias_layer[:, 8 * D : 9 * D]
    hidden_bias = lax.dynamic_slice_in_dim(
        bias_layer, 9 * D + tensor_rank * hidden_local, hidden_local, 1
    )
    last_bias = bias_layer[:, 9 * D + FF :]
    return (query_bias, value_bias, out_bias, hidden_bias, last_bias)


def forward_layer(states, weights, pieces, shifts, heads_local):
    query_bias, value_bias, out_bias, hidden_bias, last_bias = pieces
    joined = gather_streams(
        [
            modulate(states[stream], shifts[stream][0], shifts[stream][1]).astype(jnp.bfloat16)
            for stream in range(2)
        ]
    )
    columns = jnp.concatenate(
        [
            (
                jnp.dot(joined[stream], weights[0][stream], preferred_element_type=jnp.float32)
                + column_bias(query_bias[stream], value_bias[stream], heads_local)
            ).astype(jnp.bfloat16)
            for stream in range(2)
        ]
    )
    attended, logsum = attend(columns, heads_local)
    split = joined[0].shape[0]
    out_rows = [attended[:split], attended[split:]]
    summed = scatter_streams(out_rows, weights[1])[0]
    branch_attend = [summed[stream] + out_bias[stream] for stream in range(2)]
    middle = [states[stream] + shifts[stream][2] * branch_attend[stream] for stream in range(2)]
    joined_feed = gather_streams(
        [
            modulate(middle[stream], shifts[stream][3], shifts[stream][4]).astype(jnp.bfloat16)
            for stream in range(2)
        ]
    )
    preact = [
        jnp.dot(joined_feed[stream], weights[2][stream], preferred_element_type=jnp.float32)
        + hidden_bias[stream]
        for stream in range(2)
    ]
    activated = [gelu_tanh(preact[stream]).astype(jnp.bfloat16) for stream in range(2)]
    summed = scatter_streams(activated, weights[3])[0]
    branch_feed = [summed[stream] + last_bias[stream] for stream in range(2)]
    result = [middle[stream] + shifts[stream][5] * branch_feed[stream] for stream in range(2)]
    record = (
        states,
        joined,
        columns,
        attended,
        logsum,
        branch_attend,
        middle,
        joined_feed,
        preact,
        activated,
        branch_feed,
    )
    return (record, result)


def weight_grads_kernel(count, *refs):
    out_ref = refs[-1]
    offset = 0
    for index in range(count):
        left, right = refs[2 * index], refs[2 * index + 1]
        width = right.shape[1]
        tile = 384 if width % 384 == 0 else width
        for place in range(0, width, tile):
            out_ref[:, offset + place : offset + place + tile] = lax.dot_general(
                left[...],
                right[:, place : place + tile],
                contract_rows,
                preferred_element_type=jnp.float32,
            ).astype(jnp.bfloat16)
        offset += width


def weight_grads(pairs):
    tile = 256
    specs, operands, total, flops, moved = ([], [], 0, 0, 0)
    for left, right, place in pairs:
        rows, width = left.shape[0], right.shape[1]
        specs.append(pl.BlockSpec((rows, tile), lambda index: (0, index)))
        specs.append(pl.BlockSpec((rows, width), lambda index, place=place: (place, 0)))
        operands += [left, right]
        total += width
        flops += 2 * rows * width * left.shape[1]
        moved += 2 * (left.size + rows * width)
    depth = pairs[0][0].shape[1]
    return pl.pallas_call(
        functools.partial(weight_grads_kernel, len(pairs)),
        grid=(depth // tile,),
        in_specs=specs,
        out_specs=pl.BlockSpec((tile, total), lambda index: (index, 0)),
        out_shape=jax.ShapeDtypeStruct((depth, total), jnp.bfloat16),
        cost_estimate=pl.CostEstimate(
            flops=flops, bytes_accessed=moved + 2 * depth * total, transcendentals=0
        ),
        name="weight_grads",
    )(*operands)


def scatter_weights(grads):
    return lax.psum_scatter(grads, "dp", scatter_dimension=0, tiled=True)


def unpack_weights(shares, offset, width):
    return jnp.stack(
        [
            shares[:, offset + stream * width : offset + (stream + 1) * width].astype(jnp.float32)
            for stream in range(2)
        ]
    )


def backward_layer(gradients, record, weights, shifts, heads_local, pending):
    (
        states,
        joined,
        columns,
        attended,
        logsum,
        branch_attend,
        middle,
        joined_feed,
        preact,
        activated,
        branch_feed,
    ) = record
    split = joined[0].shape[0]
    out_rows = [attended[:split], attended[split:]]
    grad_branch = [shifts[stream][5] * gradients[stream] for stream in range(2)]
    gate_feed = [jnp.sum(gradients[stream] * branch_feed[stream], 0) for stream in range(2)]
    branch_rows = gather_streams([values.astype(jnp.bfloat16) for values in grad_branch])
    grad_contraction = weight_grads(
        [(branch_rows[stream], activated[stream], 0) for stream in range(2)]
    )
    branch_rows, feed_weights = after((branch_rows, weights[3]), grad_contraction, *pending[:1])
    grad_contraction = scatter_weights(grad_contraction)
    grad_preact = []
    for stream in range(2):
        grad_activated = jnp.dot(
            branch_rows[stream], feed_weights[stream], preferred_element_type=jnp.float32
        )
        gelu_back = jax.vjp(gelu_tanh, preact[stream])[1]
        grad_preact.append(gelu_back(grad_activated)[0].astype(jnp.bfloat16))
    hidden_sums = [jnp.sum(grad_preact[stream], 0, dtype=jnp.float32) for stream in range(2)]
    summed, started = scatter_streams(grad_preact, weights[2])
    behind = after(grad_preact, started)
    grad_expansion = weight_grads(
        [(joined_feed[stream], behind[stream], 0) for stream in range(2)]
    )
    summed = after(summed, grad_expansion)
    grad_expansion = scatter_weights(grad_expansion)
    grad_middle, shift_feed, scale_feed = ([], [], [])
    summed = after(summed, *pending[1:])
    for stream in range(2):
        shift_back = jax.vjp(modulate, middle[stream], shifts[stream][3], shifts[stream][4])[1]
        back_rows, back_shift, back_scale = shift_back(summed[stream])
        grad_middle.append(gradients[stream] + back_rows)
        shift_feed.append(back_shift)
        scale_feed.append(back_scale)
    grad_attend = [shifts[stream][2] * grad_middle[stream] for stream in range(2)]
    gate_attend = [jnp.sum(grad_middle[stream] * branch_attend[stream], 0) for stream in range(2)]
    attend_rows = gather_streams([values.astype(jnp.bfloat16) for values in grad_attend])
    grad_heads = jnp.concatenate(
        [
            jnp.dot(
                attend_rows[stream], weights[1][stream], preferred_element_type=jnp.float32
            ).astype(jnp.bfloat16)
            for stream in range(2)
        ]
    )
    grad_columns = attend_back(columns, attended, logsum, grad_heads, heads_local)
    column_rows = [grad_columns[:split], grad_columns[split:]]
    column_sums = [
        jnp.sum(column_rows[stream], 0, dtype=jnp.float32).reshape(heads_local, 3, HEAD_DIM)
        for stream in range(2)
    ]
    text_place = split // attend_rows[1].shape[0]

    def attention_grads(behind):
        return weight_grads(
            [
                (attend_rows[0], attended, 0),
                (attend_rows[1], attended, text_place),
                (joined[0], behind, 0),
                (joined[1], behind, text_place),
            ]
        )

    if pending:
        grad_attention = attention_grads(grad_columns)
        column_rows = after(column_rows, grad_attention)
        summed, _ = scatter_streams(column_rows, weights[0])
    else:
        summed, started = scatter_streams(column_rows, weights[0])
        grad_attention = attention_grads(after(grad_columns, started))
        summed = after(summed, grad_attention)
    computed = grad_attention
    grad_attention = scatter_weights(grad_attention)
    tensor_rank = lax.axis_index("tensor")
    width_local = heads_local * HEAD_DIM
    hidden_local = preact[0].shape[1]

    def placed(length, values, offset):
        return lax.dynamic_update_slice_in_dim(
            jnp.zeros((length,), jnp.float32), values, offset, 0
        )

    new_grads, slot_grads, bias_grads = ([], [], [])
    for stream in range(2):
        shift_back = jax.vjp(modulate, states[stream], shifts[stream][0], shifts[stream][1])[1]
        back_rows, back_shift, back_scale = shift_back(summed[stream])
        new_grads.append(grad_middle[stream] + back_rows)
        slot_grad = jnp.concatenate(
            [
                back_shift,
                back_scale,
                gate_attend[stream],
                shift_feed[stream],
                scale_feed[stream],
                gate_feed[stream],
            ]
        )
        slot_grads.append(slot_grad)
        bias_grads.append(
            jnp.concatenate(
                [
                    slot_grad,
                    placed(D, column_sums[stream][:, 0].reshape(-1), tensor_rank * width_local),
                    placed(D, column_sums[stream][:, 2].reshape(-1), tensor_rank * width_local),
                    jnp.sum(grad_attend[stream], 0),
                    placed(FF, hidden_sums[stream], tensor_rank * hidden_local),
                    jnp.sum(grad_branch[stream], 0),
                ]
            )
        )
    out_width = attended.shape[1]
    layer_grads = (
        unpack_weights(grad_attention, 2 * out_width, 3 * out_width),
        unpack_weights(grad_attention, 0, out_width),
        unpack_weights(grad_expansion, 0, hidden_local),
        unpack_weights(grad_contraction, 0, hidden_local),
    )
    pending = (grad_contraction, grad_expansion, grad_attention)
    return (
        new_grads,
        layer_grads,
        pending,
        computed,
        jnp.stack(bias_grads),
        jnp.stack(slot_grads),
    )


def slot_table(silu_rows, modulation, slots):
    size = lax.axis_size("tensor")
    rank = lax.axis_index("tensor")
    count = silu_rows.shape[0]
    partial = jnp.einsum(
        "nd,lsdm->nlsm", silu_rows, modulation.astype(jnp.float32), precision=highest
    ).reshape(count, -1)
    width = partial.shape[1] // size
    owned = 0.0
    for step in range(size):
        block = lax.dynamic_slice_in_dim(partial, (rank ^ step) * width, width, 1)
        owned = owned + (exchange(block, "tensor", step) if step else block)
    onehot = (slots[:, None] == jnp.arange(count, dtype=jnp.int32)[None, :]).astype(jnp.float32)
    per_slot = jnp.dot(onehot, owned, precision=highest)
    mine = per_slot[0]
    for step in range(1, per_slot.shape[0]):
        mine = mine + exchange(per_slot[step], "dp", step)
    table = jnp.zeros((partial.shape[1],), jnp.float32)
    for step, block in enumerate(gather_parts(mine, "tensor")):
        table = lax.dynamic_update_slice_in_dim(table, block, (rank ^ step) * width, 0)
    return table.reshape(LAYERS, 2, -1)


def on_device(
    image_tokens,
    text_tokens,
    conditioning,
    slot_sequence,
    rank_counts,
    projection,
    recombine,
    expansion,
    contraction,
    modulation,
    biases,
    cotangent_image,
    cotangent_text,
):
    tensor_rank = lax.axis_index("tensor")
    flat_rank = lax.axis_index(("dp", "tensor"))
    heads_local = HEADS // lax.axis_size("tensor")
    width_local = heads_local * HEAD_DIM
    hidden_local = FF // lax.axis_size("tensor")
    bias_all = gather_biases(biases)
    shard_rows = modulation.shape[2]
    owned_rows = lax.dynamic_slice_in_dim(
        jax.nn.silu(conditioning), flat_rank * shard_rows, shard_rows, 1
    )
    slots = jnp.concatenate(gather_parts(slot_sequence, "dp"))
    slot_shifts = slot_table(owned_rows, modulation, slots) + bias_all[:, :, : 6 * D]
    live = (rank_counts[0] > 0).astype(jnp.float32)
    states = [image_tokens.astype(jnp.float32), text_tokens.astype(jnp.float32)]
    stored = []
    for tier in range(LAYERS):
        weights = [
            lax.all_gather(matrix[tier], "dp", axis=1, tiled=True)
            for matrix in (projection, recombine, expansion, contraction)
        ]
        pieces = layer_biases(bias_all[tier], tensor_rank, width_local, hidden_local)
        shifts = [
            [slot_shifts[tier, stream, part * D : (part + 1) * D] for part in range(6)]
            for stream in range(2)
        ]
        record, states = forward_layer(states, weights, pieces, shifts, heads_local)
        stored.append((weights, shifts, record))
    gradients = [
        cotangent_image.astype(jnp.float32) * live,
        cotangent_text.astype(jnp.float32) * live,
    ]
    slot_rows = jnp.dot(
        (
            slots[:, None] == jnp.arange(conditioning.shape[0], dtype=jnp.int32)[None, :]
        ).astype(jnp.float32),
        owned_rows,
        precision=highest,
    )
    weight_store, bias_store, slot_store, modulation_store, pending = ([], [], [], [], ())
    for tier in reversed(range(LAYERS)):
        weights, shifts, record = stored[tier]
        gradients, layer_grads, pending, computed, bias_part, slot_grads = backward_layer(
            gradients, record, weights, shifts, heads_local, pending
        )
        weight_store.insert(0, layer_grads)
        bias_store.insert(0, bias_part)
        slot_store.insert(0, slot_grads)
    slot_store[1:], bias_store[1:] = after((slot_store[1:], bias_store[1:]), computed)
    for slot_grads in slot_store:
        slot_sums = jnp.stack(gather_parts(sum_over(slot_grads, "tensor"), "dp"))
        modulation_store.append(
            jnp.einsum("pd,psm->sdm", slot_rows, slot_sums, precision=highest)
        )
    stacked = [
        jnp.stack([entry[kind] for entry in weight_store]) for kind in range(4)
    ]
    biases_grad = scatter_biases(jnp.stack(bias_store), biases.shape[2])
    return (
        (states[0] * live).astype(jnp.bfloat16),
        (states[1] * live).astype(jnp.bfloat16),
        gradients[0],
        gradients[1],
        stacked[0],
        stacked[1],
        stacked[2],
        stacked[3],
        jnp.stack(modulation_store),
        biases_grad,
    )


def solution(mesh):
    in_specs = (
        P(("dp", "tensor"), None),
        P(("dp", "tensor"), None),
        P(),
        P("dp"),
        P("dp"),
        P(None, None, "dp", "tensor"),
        P(None, None, "dp", "tensor"),
        P(None, None, "dp", "tensor"),
        P(None, None, "dp", "tensor"),
        P(None, None, ("dp", "tensor"), None),
        P(None, None, ("dp", "tensor")),
        P(("dp", "tensor"), None),
        P(("dp", "tensor"), None),
    )
    out_specs = (
        P(("dp", "tensor"), None),
        P(("dp", "tensor"), None),
        P(("dp", "tensor"), None),
        P(("dp", "tensor"), None),
        P(None, None, "dp", "tensor"),
        P(None, None, "dp", "tensor"),
        P(None, None, "dp", "tensor"),
        P(None, None, "dp", "tensor"),
        P(None, None, ("dp", "tensor"), None),
        P(None, None, ("dp", "tensor")),
    )
    return jax.shard_map(
        on_device, mesh=mesh, in_specs=in_specs, out_specs=out_specs, check_vma=False
    )
```

```python
import functools
import math

import jax
import jax.numpy as jnp
from jax import lax
from jax.experimental import pallas as pl
from jax.experimental.pallas import tpu as pltpu
from jax.sharding import PartitionSpec as P

D = 1536
HEADS = 24
HEAD_DIM = 64
FF = 6144
LAYERS = 2

highest = lax.Precision.HIGHEST
contract_columns = (((1,), (1,)), ((), ()))
contract_rows = (((0,), (0,)), ((), ()))
SCALE = HEAD_DIM ** (-0.5)
EXPONENT = SCALE * math.log2(math.e)


def normalize(values):
    average = jnp.mean(values, -1, keepdims=True)
    centred = values - average
    spread = jnp.mean(centred * centred, -1, keepdims=True)
    return centred * lax.rsqrt(spread + 1e-06)


def modulate(values, shifts, scales):
    return normalize(values) * (1.0 + scales) + shifts


def gelu_tanh(values):
    return jax.nn.gelu(values, approximate=True)


def exchange(values, axis, step):
    size = lax.axis_size(axis)
    return lax.ppermute(values, axis, [(rank, rank ^ step) for rank in range(size)])


def gather_parts(values, axis):
    return [values] + [exchange(values, axis, step) for step in range(1, lax.axis_size(axis))]


def gather_rows(values, axis):
    return jnp.concatenate(gather_parts(values, axis), axis=0)


def assemble_kernel(count, *refs):
    parts, (image_ref, text_ref) = refs[:-2], refs[-2:]
    place = 0
    size = count + text_ref.shape[0] * count // image_ref.shape[0]
    for part in parts:
        rows, taken = part.shape[0], 0
        while taken < rows:
            owner, offset = divmod(place, size)
            if offset < count:
                length = min(rows - taken, count - offset)
                target, start = image_ref, owner * count + offset
            else:
                length = min(rows - taken, size - offset)
                target, start = text_ref, owner * (size - count) + offset - count
            target[start : start + length] = part[taken : taken + length]
            place, taken = place + length, taken + length


def assemble(parts, counts):
    size = lax.axis_size("tensor")
    return pl.pallas_call(
        functools.partial(assemble_kernel, counts[0]),
        out_shape=[
            jax.ShapeDtypeStruct((size * count, parts[0].shape[1]), parts[0].dtype)
            for count in counts
        ],
        cost_estimate=pl.CostEstimate(
            flops=0, bytes_accessed=4 * size * sum(counts) * parts[0].shape[1], transcendentals=0
        ),
        name="assemble",
    )(*parts)


def gather_streams(streams):
    counts = [values.shape[0] for values in streams]
    rows = jnp.concatenate(streams)
    if lax.axis_size("tensor") == 4:
        half = rows.shape[0] // 2
        first, second = (exchange(rows, "tensor", step) for step in (1, 2))
        parts = [
            rows,
            first,
            second,
            exchange(first[:half], "tensor", 2),
            exchange(second[half:], "tensor", 1),
        ]
    else:
        parts = gather_parts(rows, "tensor")
    return assemble(parts, counts)


def scatter_streams(left, right):
    size = lax.axis_size("tensor")
    counts = [values.shape[0] // size for values in left]

    def product(stream, start, stop):
        return lax.dot_general(
            left[stream][start * counts[stream] : stop * counts[stream]],
            right[stream],
            contract_columns,
            preferred_element_type=jnp.float32,
        ).astype(jnp.bfloat16)

    text = product(1, 0, size)

    def joined(image, step):
        return jnp.concatenate([image, text[step * counts[1] : (step + 1) * counts[1]]])

    if size == 4:
        half = sum(counts) // 2
        far = joined(product(0, 3, 4), 3)
        first_in = exchange(far[:half], "tensor", 1)
        second_in = exchange(far[half:], "tensor", 2)
        near = after(product(0, 1, 3), far)
        first = joined(near[: counts[0]], 1)
        second = joined(near[counts[0] :], 2)
        started = (far, near)
        first = jnp.concatenate([first[:half], first[half:] + second_in])
        second = jnp.concatenate([second[:half] + first_in, second[half:]])
        pieces = [exchange(first, "tensor", 1), exchange(second, "tensor", 2)]
    else:
        started = [joined(product(0, step, step + 1), step) for step in range(1, size)]
        pieces = [exchange(started[step - 1], "tensor", step) for step in range(1, size)]
    total = joined(product(0, 0, 1), 0).astype(jnp.float32)
    for values in pieces:
        total = total + values.astype(jnp.float32)
    return [total[: counts[0]], total[counts[0] :]], started


def sum_over(values, axis):
    total = values
    for step in range(1, lax.axis_size(axis)):
        total = total + exchange(values, axis, step)
    return total


def after(values, *needed):
    return lax.optimization_barrier((values, needed))[0]


def spread_kernel(chunks_ref, out_ref):
    count, _, width = chunks_ref.shape
    for place in range(count):
        out_ref[:, place * width : (place + 1) * width] = chunks_ref[place]


def split_kernel(values_ref, out_ref):
    count, _, width = out_ref.shape
    for place in range(count):
        out_ref[place] = values_ref[:, place * width : (place + 1) * width]


def gather_biases(biases):
    width = biases.shape[2]
    held = biases.reshape(1, LAYERS * 2, width)
    held = gather_rows(gather_rows(held, "tensor")[None], "dp")
    outer, inner = held.shape[:2]
    chunks = held.reshape(outer * inner, -1).astype(jnp.float32)
    order = (
        (jnp.arange(outer, dtype=jnp.int32) ^ lax.axis_index("dp"))[:, None] * inner
        + (jnp.arange(inner, dtype=jnp.int32) ^ lax.axis_index("tensor"))[None, :]
    ).reshape(-1)
    select = (
        order[:, None] == jnp.arange(outer * inner, dtype=jnp.int32)[None, :]
    ).astype(jnp.float32)
    ordered = jnp.dot(select, chunks, precision=highest)
    spread = pl.pallas_call(
        spread_kernel,
        out_shape=jax.ShapeDtypeStruct((LAYERS * 2, outer * inner * width), jnp.float32),
        name="spread",
    )(ordered.reshape(outer * inner, LAYERS * 2, width))
    return spread.reshape(LAYERS, 2, -1)


def scatter_biases(values, width):
    outer, inner = lax.axis_size("dp"), lax.axis_size("tensor")
    chunks = pl.pallas_call(
        split_kernel,
        out_shape=jax.ShapeDtypeStruct((outer * inner, LAYERS * 2, width), jnp.float32),
        name="split",
    )(values.reshape(LAYERS * 2, -1))
    chunks = chunks.reshape(outer, inner, LAYERS * 2, width)
    for axis, size in (("dp", outer), ("tensor", inner)):
        rank = lax.axis_index(axis)
        total = lax.dynamic_index_in_dim(chunks, rank, 0, False)
        for step in range(1, size):
            block = lax.dynamic_index_in_dim(chunks, rank ^ step, 0, False)
            total = total + exchange(block, axis, step)
        chunks = total
    return chunks.reshape(LAYERS, 2, width)


def row_block(rows):
    for block in (384, 256, 128):
        if rows % block == 0:
            return block
    return rows


def attend_kernel(heads, block, columns_ref, out_ref, log_ref):
    rows = columns_ref.shape[0]
    for head in range(heads):
        base = head * 3 * HEAD_DIM
        keys = columns_ref[:, base + HEAD_DIM : base + 2 * HEAD_DIM]
        values = columns_ref[:, base + 2 * HEAD_DIM : base + 3 * HEAD_DIM]

        def step(index, carry):
            place = pl.ds(pl.multiple_of(index * block, block), block)
            queries = columns_ref[place, base : base + HEAD_DIM]
            scores = lax.dot_general(
                queries, keys, contract_columns, preferred_element_type=jnp.float32
            )
            row_max = jnp.max(scores, -1, keepdims=True)
            weights = jnp.exp2((scores - row_max) * EXPONENT)
            totals = jnp.sum(weights, -1, keepdims=True)
            output = jnp.dot(
                weights.astype(jnp.bfloat16), values, preferred_element_type=jnp.float32
            )
            out_ref[place, head * HEAD_DIM : (head + 1) * HEAD_DIM] = (output / totals).astype(
                jnp.bfloat16
            )
            log_ref[place, head : head + 1] = row_max * EXPONENT + jnp.log2(totals)
            return carry

        lax.fori_loop(0, rows // block, step, 0)


def attend(columns, heads):
    rows = columns.shape[0]
    return pl.pallas_call(
        functools.partial(attend_kernel, heads, row_block(rows)),
        out_shape=(
            jax.ShapeDtypeStruct((rows, heads * HEAD_DIM), jnp.bfloat16),
            jax.ShapeDtypeStruct((rows, 128), jnp.float32),
        ),
        cost_estimate=pl.CostEstimate(
            flops=heads * rows * rows * HEAD_DIM * 4,
            bytes_accessed=columns.size * 3,
            transcendentals=heads * rows * rows,
        ),
        name="attend",
    )(columns)


def attend_back_kernel(
    heads, block, columns_ref, out_ref, log_ref, grad_ref, result_ref, key_acc, value_acc
):
    rows = columns_ref.shape[0]
    for head in range(heads):
        base = head * 3 * HEAD_DIM
        part = slice(head * HEAD_DIM, (head + 1) * HEAD_DIM)
        keys = columns_ref[:, base + HEAD_DIM : base + 2 * HEAD_DIM]
        values = columns_ref[:, base + 2 * HEAD_DIM : base + 3 * HEAD_DIM]
        key_acc[...] = jnp.zeros_like(key_acc)
        value_acc[...] = jnp.zeros_like(value_acc)

        def step(index, carry):
            place = pl.ds(pl.multiple_of(index * block, block), block)
            queries = columns_ref[place, base : base + HEAD_DIM]
            grad_out = grad_ref[place, part]
            inner = jnp.sum(
                grad_out.astype(jnp.float32) * out_ref[place, part].astype(jnp.float32),
                -1,
                keepdims=True,
            )
            scores = lax.dot_general(
                queries, keys, contract_columns, preferred_element_type=jnp.float32
            )
            weights = jnp.exp2(scores * EXPONENT - log_ref[place, head : head + 1])
            grad_weights = lax.dot_general(
                grad_out, values, contract_columns, preferred_element_type=jnp.float32
            )
            grad_scores = (weights * (grad_weights - inner)).astype(jnp.bfloat16)
            result_ref[place, base : base + HEAD_DIM] = (
                jnp.dot(grad_scores, keys, preferred_element_type=jnp.float32) * SCALE
            ).astype(jnp.bfloat16)
            key_acc[...] += lax.dot_general(
                grad_scores, queries, contract_rows, preferred_element_type=jnp.float32
            )
            value_acc[...] += lax.dot_general(
                weights.astype(jnp.bfloat16),
                grad_out,
                contract_rows,
                preferred_element_type=jnp.float32,
            )
            return carry

        lax.fori_loop(0, rows // block, step, 0)
        result_ref[:, base + HEAD_DIM : base + 2 * HEAD_DIM] = (key_acc[...] * SCALE).astype(
            jnp.bfloat16
        )
        result_ref[:, base + 2 * HEAD_DIM : base + 3 * HEAD_DIM] = value_acc[...].astype(
            jnp.bfloat16
        )


def attend_back(columns, output, logsum, grad_output, heads):
    rows = columns.shape[0]
    return pl.pallas_call(
        functools.partial(attend_back_kernel, heads, row_block(rows)),
        out_shape=jax.ShapeDtypeStruct(columns.shape, jnp.bfloat16),
        scratch_shapes=[
            pltpu.VMEM((rows, HEAD_DIM), jnp.float32),
            pltpu.VMEM((rows, HEAD_DIM), jnp.float32),
        ],
        cost_estimate=pl.CostEstimate(
            flops=heads * rows * rows * HEAD_DIM * 10,
            bytes_accessed=columns.size * 6,
            transcendentals=heads * rows * rows,
        ),
        name="attend_back",
    )(columns, output, logsum, grad_output)


def column_bias(query_bias, value_bias, heads):
    query_part = query_bias.reshape(heads, HEAD_DIM)
    value_part = value_bias.reshape(heads, HEAD_DIM)
    return jnp.stack([query_part, jnp.zeros_like(query_part), value_part], axis=1).reshape(-1)


def layer_biases(bias_layer, tensor_rank, width_local, hidden_local):
    query_bias = lax.dynamic_slice_in_dim(
        bias_layer, 6 * D + tensor_rank * width_local, width_local, 1
    )
    value_bias = lax.dynamic_slice_in_dim(
        bias_layer, 7 * D + tensor_rank * width_local, width_local, 1
    )
    out_bias = bias_layer[:, 8 * D : 9 * D]
    hidden_bias = lax.dynamic_slice_in_dim(
        bias_layer, 9 * D + tensor_rank * hidden_local, hidden_local, 1
    )
    last_bias = bias_layer[:, 9 * D + FF :]
    return (query_bias, value_bias, out_bias, hidden_bias, last_bias)


def forward_layer(states, weights, pieces, shifts, heads_local):
    query_bias, value_bias, out_bias, hidden_bias, last_bias = pieces
    joined = gather_streams(
        [
            modulate(states[stream], shifts[stream][0], shifts[stream][1]).astype(jnp.bfloat16)
            for stream in range(2)
        ]
    )
    columns = jnp.concatenate(
        [
            (
                jnp.dot(joined[stream], weights[0][stream], preferred_element_type=jnp.float32)
                + column_bias(query_bias[stream], value_bias[stream], heads_local)
            ).astype(jnp.bfloat16)
            for stream in range(2)
        ]
    )
    attended, logsum = attend(columns, heads_local)
    split = joined[0].shape[0]
    out_rows = [attended[:split], attended[split:]]
    summed = scatter_streams(out_rows, weights[1])[0]
    branch_attend = [summed[stream] + out_bias[stream] for stream in range(2)]
    middle = [states[stream] + shifts[stream][2] * branch_attend[stream] for stream in range(2)]
    joined_feed = gather_streams(
        [
            modulate(middle[stream], shifts[stream][3], shifts[stream][4]).astype(jnp.bfloat16)
            for stream in range(2)
        ]
    )
    preact = [
        jnp.dot(joined_feed[stream], weights[2][stream], preferred_element_type=jnp.float32)
        + hidden_bias[stream]
        for stream in range(2)
    ]
    activated = [gelu_tanh(preact[stream]).astype(jnp.bfloat16) for stream in range(2)]
    summed = scatter_streams(activated, weights[3])[0]
    branch_feed = [summed[stream] + last_bias[stream] for stream in range(2)]
    result = [middle[stream] + shifts[stream][5] * branch_feed[stream] for stream in range(2)]
    record = (
        states,
        joined,
        columns,
        attended,
        logsum,
        branch_attend,
        middle,
        joined_feed,
        preact,
        activated,
        branch_feed,
    )
    return (record, result)


def weight_grads_kernel(count, *refs):
    out_ref = refs[-1]
    offset = 0
    for index in range(count):
        left, right = refs[2 * index], refs[2 * index + 1]
        width = right.shape[1]
        tile = 384 if width % 384 == 0 else width
        for place in range(0, width, tile):
            out_ref[:, offset + place : offset + place + tile] = lax.dot_general(
                left[...],
                right[:, place : place + tile],
                contract_rows,
                preferred_element_type=jnp.float32,
            ).astype(jnp.bfloat16)
        offset += width


def weight_grads(pairs):
    tile = 256
    specs, operands, total, flops, moved = ([], [], 0, 0, 0)
    for left, right, place in pairs:
        rows, width = left.shape[0], right.shape[1]
        specs.append(pl.BlockSpec((rows, tile), lambda index: (0, index)))
        specs.append(pl.BlockSpec((rows, width), lambda index, place=place: (place, 0)))
        operands += [left, right]
        total += width
        flops += 2 * rows * width * left.shape[1]
        moved += 2 * (left.size + rows * width)
    depth = pairs[0][0].shape[1]
    return pl.pallas_call(
        functools.partial(weight_grads_kernel, len(pairs)),
        grid=(depth // tile,),
        in_specs=specs,
        out_specs=pl.BlockSpec((tile, total), lambda index: (index, 0)),
        out_shape=jax.ShapeDtypeStruct((depth, total), jnp.bfloat16),
        cost_estimate=pl.CostEstimate(
            flops=flops, bytes_accessed=moved + 2 * depth * total, transcendentals=0
        ),
        name="weight_grads",
    )(*operands)


def scatter_weights(grads):
    return lax.psum_scatter(grads, "dp", scatter_dimension=0, tiled=True)


def unpack_weights(shares, offset, width):
    return jnp.stack(
        [
            shares[:, offset + stream * width : offset + (stream + 1) * width].astype(jnp.float32)
            for stream in range(2)
        ]
    )


def backward_layer(gradients, record, weights, shifts, heads_local, pending):
    (
        states,
        joined,
        columns,
        attended,
        logsum,
        branch_attend,
        middle,
        joined_feed,
        preact,
        activated,
        branch_feed,
    ) = record
    split = joined[0].shape[0]
    out_rows = [attended[:split], attended[split:]]
    grad_branch = [shifts[stream][5] * gradients[stream] for stream in range(2)]
    gate_feed = [jnp.sum(gradients[stream] * branch_feed[stream], 0) for stream in range(2)]
    branch_rows = gather_streams([values.astype(jnp.bfloat16) for values in grad_branch])
    grad_contraction = weight_grads(
        [(branch_rows[stream], activated[stream], 0) for stream in range(2)]
    )
    branch_rows, feed_weights = after((branch_rows, weights[3]), grad_contraction, *pending[:1])
    grad_contraction = scatter_weights(grad_contraction)
    grad_preact = []
    for stream in range(2):
        grad_activated = jnp.dot(
            branch_rows[stream], feed_weights[stream], preferred_element_type=jnp.float32
        )
        gelu_back = jax.vjp(gelu_tanh, preact[stream])[1]
        grad_preact.append(gelu_back(grad_activated)[0].astype(jnp.bfloat16))
    hidden_sums = [jnp.sum(grad_preact[stream], 0, dtype=jnp.float32) for stream in range(2)]
    summed, started = scatter_streams(grad_preact, weights[2])
    behind = after(grad_preact, started)
    grad_expansion = weight_grads(
        [(joined_feed[stream], behind[stream], 0) for stream in range(2)]
    )
    summed = after(summed, grad_expansion)
    grad_expansion = scatter_weights(grad_expansion)
    grad_middle, shift_feed, scale_feed = ([], [], [])
    summed = after(summed, *pending[1:])
    for stream in range(2):
        shift_back = jax.vjp(modulate, middle[stream], shifts[stream][3], shifts[stream][4])[1]
        back_rows, back_shift, back_scale = shift_back(summed[stream])
        grad_middle.append(gradients[stream] + back_rows)
        shift_feed.append(back_shift)
        scale_feed.append(back_scale)
    grad_attend = [shifts[stream][2] * grad_middle[stream] for stream in range(2)]
    gate_attend = [jnp.sum(grad_middle[stream] * branch_attend[stream], 0) for stream in range(2)]
    attend_rows = gather_streams([values.astype(jnp.bfloat16) for values in grad_attend])
    grad_heads = jnp.concatenate(
        [
            jnp.dot(
                attend_rows[stream], weights[1][stream], preferred_element_type=jnp.float32
            ).astype(jnp.bfloat16)
            for stream in range(2)
        ]
    )
    grad_columns = attend_back(columns, attended, logsum, grad_heads, heads_local)
    column_rows = [grad_columns[:split], grad_columns[split:]]
    column_sums = [
        jnp.sum(column_rows[stream], 0, dtype=jnp.float32).reshape(heads_local, 3, HEAD_DIM)
        for stream in range(2)
    ]
    text_place = split // attend_rows[1].shape[0]

    def attention_grads(behind):
        return weight_grads(
            [
                (attend_rows[0], attended, 0),
                (attend_rows[1], attended, text_place),
                (joined[0], behind, 0),
                (joined[1], behind, text_place),
            ]
        )

    if pending:
        grad_attention = attention_grads(grad_columns)
        column_rows = after(column_rows, grad_attention)
        summed, _ = scatter_streams(column_rows, weights[0])
    else:
        summed, started = scatter_streams(column_rows, weights[0])
        grad_attention = attention_grads(after(grad_columns, started))
        summed = after(summed, grad_attention)
    computed = grad_attention
    grad_attention = scatter_weights(grad_attention)
    tensor_rank = lax.axis_index("tensor")
    width_local = heads_local * HEAD_DIM
    hidden_local = preact[0].shape[1]

    def placed(length, values, offset):
        return lax.dynamic_update_slice_in_dim(
            jnp.zeros((length,), jnp.float32), values, offset, 0
        )

    new_grads, slot_grads, bias_grads = ([], [], [])
    for stream in range(2):
        shift_back = jax.vjp(modulate, states[stream], shifts[stream][0], shifts[stream][1])[1]
        back_rows, back_shift, back_scale = shift_back(summed[stream])
        new_grads.append(grad_middle[stream] + back_rows)
        slot_grad = jnp.concatenate(
            [
                back_shift,
                back_scale,
                gate_attend[stream],
                shift_feed[stream],
                scale_feed[stream],
                gate_feed[stream],
            ]
        )
        slot_grads.append(slot_grad)
        bias_grads.append(
            jnp.concatenate(
                [
                    slot_grad,
                    placed(D, column_sums[stream][:, 0].reshape(-1), tensor_rank * width_local),
                    placed(D, column_sums[stream][:, 2].reshape(-1), tensor_rank * width_local),
                    jnp.sum(grad_attend[stream], 0),
                    placed(FF, hidden_sums[stream], tensor_rank * hidden_local),
                    jnp.sum(grad_branch[stream], 0),
                ]
            )
        )
    out_width = attended.shape[1]
    layer_grads = (
        unpack_weights(grad_attention, 2 * out_width, 3 * out_width),
        unpack_weights(grad_attention, 0, out_width),
        unpack_weights(grad_expansion, 0, hidden_local),
        unpack_weights(grad_contraction, 0, hidden_local),
    )
    pending = (grad_contraction, grad_expansion, grad_attention)
    return (
        new_grads,
        layer_grads,
        pending,
        computed,
        jnp.stack(bias_grads),
        jnp.stack(slot_grads),
    )


def slot_table(silu_rows, modulation, slots):
    size = lax.axis_size("tensor")
    rank = lax.axis_index("tensor")
    count = silu_rows.shape[0]
    partial = jnp.einsum(
        "nd,lsdm->nlsm", silu_rows, modulation.astype(jnp.float32), precision=highest
    ).reshape(count, -1)
    width = partial.shape[1] // size
    owned = 0.0
    for step in range(size):
        block = lax.dynamic_slice_in_dim(partial, (rank ^ step) * width, width, 1)
        owned = owned + (exchange(block, "tensor", step) if step else block)
    onehot = (slots[:, None] == jnp.arange(count, dtype=jnp.int32)[None, :]).astype(jnp.float32)
    per_slot = jnp.dot(onehot, owned, precision=highest)
    mine = per_slot[0]
    for step in range(1, per_slot.shape[0]):
        mine = mine + exchange(per_slot[step], "dp", step)
    table = jnp.zeros((partial.shape[1],), jnp.float32)
    for step, block in enumerate(gather_parts(mine, "tensor")):
        table = lax.dynamic_update_slice_in_dim(table, block, (rank ^ step) * width, 0)
    return table.reshape(LAYERS, 2, -1)


def gather_slots(slot_grads):
    size = lax.axis_size("tensor")
    rank = lax.axis_index("tensor")
    values = slot_grads.reshape(size, 1, -1)
    owned = lax.dynamic_index_in_dim(values, rank, 0, False)
    for step in range(1, size):
        block = lax.dynamic_index_in_dim(values, rank ^ step, 0, False)
        owned = owned + exchange(block, "tensor", step)
    owned = gather_rows(owned, "dp")
    result = jnp.zeros((owned.shape[0], size * owned.shape[1]), jnp.float32)
    for step, block in enumerate(gather_parts(owned, "tensor")):
        result = lax.dynamic_update_slice_in_dim(result, block, (rank ^ step) * owned.shape[1], 1)
    return result


def on_device(
    image_tokens,
    text_tokens,
    conditioning,
    slot_sequence,
    rank_counts,
    projection,
    recombine,
    expansion,
    contraction,
    modulation,
    biases,
    cotangent_image,
    cotangent_text,
):
    tensor_rank = lax.axis_index("tensor")
    flat_rank = lax.axis_index(("dp", "tensor"))
    heads_local = HEADS // lax.axis_size("tensor")
    width_local = heads_local * HEAD_DIM
    hidden_local = FF // lax.axis_size("tensor")
    bias_all = gather_biases(biases)
    shard_rows = modulation.shape[2]
    owned_rows = lax.dynamic_slice_in_dim(
        jax.nn.silu(conditioning), flat_rank * shard_rows, shard_rows, 1
    )
    slots = jnp.concatenate(gather_parts(slot_sequence, "dp"))
    slot_shifts = slot_table(owned_rows, modulation, slots) + bias_all[:, :, : 6 * D]
    live = (rank_counts[0] > 0).astype(jnp.float32)
    states = [image_tokens.astype(jnp.float32), text_tokens.astype(jnp.float32)]
    stored = []
    for tier in range(LAYERS):
        attention, up, down = [
            lax.all_gather(matrix, "dp", axis=1, tiled=True)
            for matrix in (
                jnp.concatenate([projection[tier], recombine[tier]], axis=2),
                expansion[tier],
                contraction[tier],
            )
        ]
        width = projection.shape[3]
        weights = [attention[:, :, :width], attention[:, :, width:], up, down]
        pieces = layer_biases(bias_all[tier], tensor_rank, width_local, hidden_local)
        shifts = [
            [slot_shifts[tier, stream, part * D : (part + 1) * D] for part in range(6)]
            for stream in range(2)
        ]
        record, states = forward_layer(states, weights, pieces, shifts, heads_local)
        stored.append((weights, shifts, record))
    gradients = [
        cotangent_image.astype(jnp.float32) * live,
        cotangent_text.astype(jnp.float32) * live,
    ]
    slot_rows = jnp.dot(
        (
            slots[:, None] == jnp.arange(conditioning.shape[0], dtype=jnp.int32)[None, :]
        ).astype(jnp.float32),
        owned_rows,
        precision=highest,
    )
    weight_store, bias_store, slot_store, modulation_store, pending = ([], [], [], [], ())
    for tier in reversed(range(LAYERS)):
        weights, shifts, record = stored[tier]
        gradients, layer_grads, pending, computed, bias_part, slot_grads = backward_layer(
            gradients, record, weights, shifts, heads_local, pending
        )
        weight_store.insert(0, layer_grads)
        bias_store.insert(0, bias_part)
        slot_store.insert(0, slot_grads)
    slot_store[1:], bias_store[1:] = after((slot_store[1:], bias_store[1:]), computed)
    for slot_grads in slot_store:
        modulation_store.append(
            jnp.dot(slot_rows.T, gather_slots(slot_grads), precision=highest)
            .reshape(shard_rows, 2, -1)
            .transpose(1, 0, 2)
        )
    stacked = [
        jnp.stack([entry[kind] for entry in weight_store]) for kind in range(4)
    ]
    biases_grad = scatter_biases(jnp.stack(bias_store), biases.shape[2])
    return (
        (states[0] * live).astype(jnp.bfloat16),
        (states[1] * live).astype(jnp.bfloat16),
        gradients[0],
        gradients[1],
        stacked[0],
        stacked[1],
        stacked[2],
        stacked[3],
        jnp.stack(modulation_store),
        biases_grad,
    )


def solution(mesh):
    in_specs = (
        P(("dp", "tensor"), None),
        P(("dp", "tensor"), None),
        P(),
        P("dp"),
        P("dp"),
        P(None, None, "dp", "tensor"),
        P(None, None, "dp", "tensor"),
        P(None, None, "dp", "tensor"),
        P(None, None, "dp", "tensor"),
        P(None, None, ("dp", "tensor"), None),
        P(None, None, ("dp", "tensor")),
        P(("dp", "tensor"), None),
        P(("dp", "tensor"), None),
    )
    out_specs = (
        P(("dp", "tensor"), None),
        P(("dp", "tensor"), None),
        P(("dp", "tensor"), None),
        P(("dp", "tensor"), None),
        P(None, None, "dp", "tensor"),
        P(None, None, "dp", "tensor"),
        P(None, None, "dp", "tensor"),
        P(None, None, "dp", "tensor"),
        P(None, None, ("dp", "tensor"), None),
        P(None, None, ("dp", "tensor")),
    )
    return jax.shard_map(
        on_device, mesh=mesh, in_specs=in_specs, out_specs=out_specs, check_vma=False
    )
```

```python
import functools
import math

import jax
import jax.numpy as jnp
from jax import lax
from jax.experimental import pallas as pl
from jax.experimental.pallas import tpu as pltpu
from jax.sharding import PartitionSpec as P

D = 1536
HEADS = 24
HEAD_DIM = 64
FF = 6144
LAYERS = 2

highest = lax.Precision.HIGHEST
contract_columns = (((1,), (1,)), ((), ()))
contract_rows = (((0,), (0,)), ((), ()))
SCALE = HEAD_DIM ** (-0.5)
EXPONENT = SCALE * math.log2(math.e)


def normalize(values):
    average = jnp.mean(values, -1, keepdims=True)
    centred = values - average
    spread = jnp.mean(centred * centred, -1, keepdims=True)
    return centred * lax.rsqrt(spread + 1e-06)


def modulate(values, shifts, scales):
    return normalize(values) * (1.0 + scales) + shifts


def gelu_tanh(values):
    return jax.nn.gelu(values, approximate=True)


def exchange(values, axis, step):
    size = lax.axis_size(axis)
    return lax.ppermute(values, axis, [(rank, rank ^ step) for rank in range(size)])


def gather_parts(values, axis):
    return [values] + [exchange(values, axis, step) for step in range(1, lax.axis_size(axis))]


def gather_rows(values, axis):
    return jnp.concatenate(gather_parts(values, axis), axis=0)


def assemble_kernel(count, *refs):
    parts, (image_ref, text_ref) = refs[:-2], refs[-2:]
    place = 0
    size = count + text_ref.shape[0] * count // image_ref.shape[0]
    for part in parts:
        rows, taken = part.shape[0], 0
        while taken < rows:
            owner, offset = divmod(place, size)
            if offset < count:
                length = min(rows - taken, count - offset)
                target, start = image_ref, owner * count + offset
            else:
                length = min(rows - taken, size - offset)
                target, start = text_ref, owner * (size - count) + offset - count
            target[start : start + length] = part[taken : taken + length]
            place, taken = place + length, taken + length


def assemble(parts, counts):
    size = lax.axis_size("tensor")
    return pl.pallas_call(
        functools.partial(assemble_kernel, counts[0]),
        out_shape=[
            jax.ShapeDtypeStruct((size * count, parts[0].shape[1]), parts[0].dtype)
            for count in counts
        ],
        cost_estimate=pl.CostEstimate(
            flops=0, bytes_accessed=4 * size * sum(counts) * parts[0].shape[1], transcendentals=0
        ),
        name="assemble",
    )(*parts)


def gather_streams(streams):
    counts = [values.shape[0] for values in streams]
    rows = jnp.concatenate(streams)
    if lax.axis_size("tensor") == 4:
        half = rows.shape[0] // 2
        first, second = (exchange(rows, "tensor", step) for step in (1, 2))
        parts = [
            rows,
            first,
            second,
            exchange(first[:half], "tensor", 2),
            exchange(second[half:], "tensor", 1),
        ]
    else:
        parts = gather_parts(rows, "tensor")
    return assemble(parts, counts)


def scatter_streams(left, right):
    size = lax.axis_size("tensor")
    counts = [values.shape[0] // size for values in left]

    def product(stream, start, stop):
        return lax.dot_general(
            left[stream][start * counts[stream] : stop * counts[stream]],
            right[stream],
            contract_columns,
            preferred_element_type=jnp.float32,
        ).astype(jnp.bfloat16)

    text = product(1, 0, size)

    def joined(image, step):
        return jnp.concatenate([image, text[step * counts[1] : (step + 1) * counts[1]]])

    if size == 4:
        half = sum(counts) // 2
        far = joined(product(0, 3, 4), 3)
        first_in = exchange(far[:half], "tensor", 1)
        second_in = exchange(far[half:], "tensor", 2)
        near = after(product(0, 1, 3), far)
        first = joined(near[: counts[0]], 1)
        second = joined(near[counts[0] :], 2)
        started = (far, near)
        first = jnp.concatenate([first[:half], first[half:] + second_in])
        second = jnp.concatenate([second[:half] + first_in, second[half:]])
        pieces = [exchange(first, "tensor", 1), exchange(second, "tensor", 2)]
    else:
        started = [joined(product(0, step, step + 1), step) for step in range(1, size)]
        pieces = [exchange(started[step - 1], "tensor", step) for step in range(1, size)]
    total = joined(product(0, 0, 1), 0).astype(jnp.float32)
    for values in pieces:
        total = total + values.astype(jnp.float32)
    return [total[: counts[0]], total[counts[0] :]], started


def sum_over(values, axis):
    total = values
    for step in range(1, lax.axis_size(axis)):
        total = total + exchange(values, axis, step)
    return total


def after(values, *needed):
    return lax.optimization_barrier((values, needed))[0]


def spread_kernel(chunks_ref, out_ref):
    count, _, width = chunks_ref.shape
    for place in range(count):
        out_ref[:, place * width : (place + 1) * width] = chunks_ref[place]


def split_kernel(values_ref, out_ref):
    count, _, width = out_ref.shape
    for place in range(count):
        out_ref[place] = values_ref[:, place * width : (place + 1) * width]


def gather_biases(biases):
    width = biases.shape[2]
    held = biases.reshape(1, LAYERS * 2, width)
    held = gather_rows(gather_rows(held, "tensor")[None], "dp")
    outer, inner = held.shape[:2]
    chunks = held.reshape(outer * inner, -1).astype(jnp.float32)
    order = (
        (jnp.arange(outer, dtype=jnp.int32) ^ lax.axis_index("dp"))[:, None] * inner
        + (jnp.arange(inner, dtype=jnp.int32) ^ lax.axis_index("tensor"))[None, :]
    ).reshape(-1)
    select = (
        order[:, None] == jnp.arange(outer * inner, dtype=jnp.int32)[None, :]
    ).astype(jnp.float32)
    ordered = jnp.dot(select, chunks, precision=highest)
    spread = pl.pallas_call(
        spread_kernel,
        out_shape=jax.ShapeDtypeStruct((LAYERS * 2, outer * inner * width), jnp.float32),
        name="spread",
    )(ordered.reshape(outer * inner, LAYERS * 2, width))
    return spread.reshape(LAYERS, 2, -1)


def scatter_biases(values, width):
    outer, inner = lax.axis_size("dp"), lax.axis_size("tensor")
    chunks = pl.pallas_call(
        split_kernel,
        out_shape=jax.ShapeDtypeStruct((outer * inner, LAYERS * 2, width), jnp.float32),
        name="split",
    )(values.reshape(LAYERS * 2, -1))
    chunks = chunks.reshape(outer, inner, LAYERS * 2, width)
    for axis, size in (("dp", outer), ("tensor", inner)):
        rank = lax.axis_index(axis)
        total = lax.dynamic_index_in_dim(chunks, rank, 0, False)
        for step in range(1, size):
            block = lax.dynamic_index_in_dim(chunks, rank ^ step, 0, False)
            total = total + exchange(block, axis, step)
        chunks = total
    return chunks.reshape(LAYERS, 2, width)


def attend_kernel(heads, columns_ref, out_ref, log_ref):
    for head in range(heads):
        base = head * 3 * HEAD_DIM
        queries = columns_ref[:, base : base + HEAD_DIM]
        keys = columns_ref[:, base + HEAD_DIM : base + 2 * HEAD_DIM]
        values = columns_ref[:, base + 2 * HEAD_DIM : base + 3 * HEAD_DIM]
        scores = lax.dot_general(
            queries, keys, contract_columns, preferred_element_type=jnp.float32
        )
        row_max = jnp.max(scores, -1, keepdims=True)
        weights = jnp.exp2((scores - row_max) * EXPONENT)
        totals = jnp.sum(weights, -1, keepdims=True)
        output = jnp.dot(weights.astype(jnp.bfloat16), values, preferred_element_type=jnp.float32)
        out_ref[:, head * HEAD_DIM : (head + 1) * HEAD_DIM] = (output / totals).astype(
            jnp.bfloat16
        )
        log_ref[:, head : head + 1] = row_max * EXPONENT + jnp.log2(totals)


def attend(columns, heads):
    rows = columns.shape[0]
    return pl.pallas_call(
        functools.partial(attend_kernel, heads),
        out_shape=(
            jax.ShapeDtypeStruct((rows, heads * HEAD_DIM), jnp.bfloat16),
            jax.ShapeDtypeStruct((rows, 128), jnp.float32),
        ),
        cost_estimate=pl.CostEstimate(
            flops=heads * rows * rows * HEAD_DIM * 4,
            bytes_accessed=columns.size * 3,
            transcendentals=heads * rows * rows,
        ),
        name="attend",
    )(columns)


def attend_back_kernel(heads, columns_ref, out_ref, log_ref, grad_ref, result_ref):
    for head in range(heads):
        base = head * 3 * HEAD_DIM
        part = slice(head * HEAD_DIM, (head + 1) * HEAD_DIM)
        queries = columns_ref[:, base : base + HEAD_DIM]
        keys = columns_ref[:, base + HEAD_DIM : base + 2 * HEAD_DIM]
        values = columns_ref[:, base + 2 * HEAD_DIM : base + 3 * HEAD_DIM]
        grad_out = grad_ref[:, part]
        inner = jnp.sum(
            grad_out.astype(jnp.float32) * out_ref[:, part].astype(jnp.float32),
            -1,
            keepdims=True,
        )
        scores = lax.dot_general(
            queries, keys, contract_columns, preferred_element_type=jnp.float32
        )
        weights = jnp.exp2(scores * EXPONENT - log_ref[:, head : head + 1])
        grad_weights = lax.dot_general(
            grad_out, values, contract_columns, preferred_element_type=jnp.float32
        )
        grad_scores = (weights * (grad_weights - inner)).astype(jnp.bfloat16)
        grad_queries = jnp.dot(grad_scores, keys, preferred_element_type=jnp.float32)
        grad_keys = lax.dot_general(
            grad_scores, queries, contract_rows, preferred_element_type=jnp.float32
        )
        grad_values = lax.dot_general(
            weights.astype(jnp.bfloat16),
            grad_out,
            contract_rows,
            preferred_element_type=jnp.float32,
        )
        result_ref[:, base : base + HEAD_DIM] = (grad_queries * SCALE).astype(jnp.bfloat16)
        result_ref[:, base + HEAD_DIM : base + 2 * HEAD_DIM] = (grad_keys * SCALE).astype(
            jnp.bfloat16
        )
        result_ref[:, base + 2 * HEAD_DIM : base + 3 * HEAD_DIM] = grad_values.astype(
            jnp.bfloat16
        )


def attend_back(columns, output, logsum, grad_output, heads):
    rows = columns.shape[0]
    return pl.pallas_call(
        functools.partial(attend_back_kernel, heads),
        out_shape=jax.ShapeDtypeStruct(columns.shape, jnp.bfloat16),
        cost_estimate=pl.CostEstimate(
            flops=heads * rows * rows * HEAD_DIM * 10,
            bytes_accessed=columns.size * 6,
            transcendentals=heads * rows * rows,
        ),
        name="attend_back",
    )(columns, output, logsum, grad_output)


def column_bias(query_bias, value_bias, heads):
    query_part = query_bias.reshape(heads, HEAD_DIM)
    value_part = value_bias.reshape(heads, HEAD_DIM)
    return jnp.stack([query_part, jnp.zeros_like(query_part), value_part], axis=1).reshape(-1)


def layer_biases(bias_layer, tensor_rank, width_local, hidden_local):
    query_bias = lax.dynamic_slice_in_dim(
        bias_layer, 6 * D + tensor_rank * width_local, width_local, 1
    )
    value_bias = lax.dynamic_slice_in_dim(
        bias_layer, 7 * D + tensor_rank * width_local, width_local, 1
    )
    out_bias = bias_layer[:, 8 * D : 9 * D]
    hidden_bias = lax.dynamic_slice_in_dim(
        bias_layer, 9 * D + tensor_rank * hidden_local, hidden_local, 1
    )
    last_bias = bias_layer[:, 9 * D + FF :]
    return (query_bias, value_bias, out_bias, hidden_bias, last_bias)


def forward_layer(states, weights, pieces, shifts, heads_local):
    query_bias, value_bias, out_bias, hidden_bias, last_bias = pieces
    joined = gather_streams(
        [
            modulate(states[stream], shifts[stream][0], shifts[stream][1]).astype(jnp.bfloat16)
            for stream in range(2)
        ]
    )
    columns = jnp.concatenate(
        [
            (
                jnp.dot(joined[stream], weights[0][stream], preferred_element_type=jnp.float32)
                + column_bias(query_bias[stream], value_bias[stream], heads_local)
            ).astype(jnp.bfloat16)
            for stream in range(2)
        ]
    )
    attended, logsum = attend(columns, heads_local)
    split = joined[0].shape[0]
    out_rows = [attended[:split], attended[split:]]
    summed = scatter_streams(out_rows, weights[1])[0]
    branch_attend = [summed[stream] + out_bias[stream] for stream in range(2)]
    middle = [states[stream] + shifts[stream][2] * branch_attend[stream] for stream in range(2)]
    joined_feed = gather_streams(
        [
            modulate(middle[stream], shifts[stream][3], shifts[stream][4]).astype(jnp.bfloat16)
            for stream in range(2)
        ]
    )
    preact = [
        jnp.dot(joined_feed[stream], weights[2][stream], preferred_element_type=jnp.float32)
        + hidden_bias[stream]
        for stream in range(2)
    ]
    activated = [gelu_tanh(preact[stream]).astype(jnp.bfloat16) for stream in range(2)]
    summed = scatter_streams(activated, weights[3])[0]
    branch_feed = [summed[stream] + last_bias[stream] for stream in range(2)]
    result = [middle[stream] + shifts[stream][5] * branch_feed[stream] for stream in range(2)]
    record = (
        states,
        joined,
        columns,
        attended,
        logsum,
        branch_attend,
        middle,
        joined_feed,
        preact,
        activated,
        branch_feed,
    )
    return (record, result)


def weight_grads_kernel(count, *refs):
    out_ref = refs[-1]
    offset = 0
    for index in range(count):
        left, right = refs[2 * index], refs[2 * index + 1]
        width = right.shape[1]
        tile = 384 if width % 384 == 0 else width
        for place in range(0, width, tile):
            out_ref[:, offset + place : offset + place + tile] = lax.dot_general(
                left[...],
                right[:, place : place + tile],
                contract_rows,
                preferred_element_type=jnp.float32,
            ).astype(jnp.bfloat16)
        offset += width


def weight_grads(pairs):
    tile = 256
    specs, operands, total, flops, moved = ([], [], 0, 0, 0)
    for left, right, place in pairs:
        rows, width = left.shape[0], right.shape[1]
        specs.append(pl.BlockSpec((rows, tile), lambda index: (0, index)))
        specs.append(pl.BlockSpec((rows, width), lambda index, place=place: (place, 0)))
        operands += [left, right]
        total += width
        flops += 2 * rows * width * left.shape[1]
        moved += 2 * (left.size + rows * width)
    depth = pairs[0][0].shape[1]
    return pl.pallas_call(
        functools.partial(weight_grads_kernel, len(pairs)),
        grid=(depth // tile,),
        in_specs=specs,
        out_specs=pl.BlockSpec((tile, total), lambda index: (index, 0)),
        out_shape=jax.ShapeDtypeStruct((depth, total), jnp.bfloat16),
        cost_estimate=pl.CostEstimate(
            flops=flops, bytes_accessed=moved + 2 * depth * total, transcendentals=0
        ),
        name="weight_grads",
    )(*operands)


def scatter_weights(grads):
    return lax.psum_scatter(grads, "dp", scatter_dimension=0, tiled=True)


def unpack_weights(shares, offset, width):
    return jnp.stack(
        [
            shares[:, offset + stream * width : offset + (stream + 1) * width].astype(jnp.float32)
            for stream in range(2)
        ]
    )


def backward_layer(gradients, record, weights, shifts, heads_local, pending):
    (
        states,
        joined,
        columns,
        attended,
        logsum,
        branch_attend,
        middle,
        joined_feed,
        preact,
        activated,
        branch_feed,
    ) = record
    split = joined[0].shape[0]
    out_rows = [attended[:split], attended[split:]]
    grad_branch = [shifts[stream][5] * gradients[stream] for stream in range(2)]
    gate_feed = [jnp.sum(gradients[stream] * branch_feed[stream], 0) for stream in range(2)]
    branch_rows = gather_streams([values.astype(jnp.bfloat16) for values in grad_branch])
    grad_contraction = weight_grads(
        [(branch_rows[stream], activated[stream], 0) for stream in range(2)]
    )
    branch_rows, feed_weights = after((branch_rows, weights[3]), grad_contraction, *pending[:1])
    grad_contraction = scatter_weights(grad_contraction)
    grad_preact = []
    for stream in range(2):
        grad_activated = jnp.dot(
            branch_rows[stream], feed_weights[stream], preferred_element_type=jnp.float32
        )
        gelu_back = jax.vjp(gelu_tanh, preact[stream])[1]
        grad_preact.append(gelu_back(grad_activated)[0].astype(jnp.bfloat16))
    hidden_sums = [jnp.sum(grad_preact[stream], 0, dtype=jnp.float32) for stream in range(2)]
    summed, started = scatter_streams(grad_preact, weights[2])
    behind = after(grad_preact, started)
    factors = [(joined_feed[stream], behind[stream], 0) for stream in range(2)]
    grad_expansion = weight_grads(factors)
    summed = after(summed, grad_expansion)
    grad_expansion = scatter_weights(grad_expansion)
    grad_middle, shift_feed, scale_feed = ([], [], [])
    summed = after(summed, *pending[1:])
    for stream in range(2):
        shift_back = jax.vjp(modulate, middle[stream], shifts[stream][3], shifts[stream][4])[1]
        back_rows, back_shift, back_scale = shift_back(summed[stream])
        grad_middle.append(gradients[stream] + back_rows)
        shift_feed.append(back_shift)
        scale_feed.append(back_scale)
    grad_attend = [shifts[stream][2] * grad_middle[stream] for stream in range(2)]
    gate_attend = [jnp.sum(grad_middle[stream] * branch_attend[stream], 0) for stream in range(2)]
    attend_rows = gather_streams([values.astype(jnp.bfloat16) for values in grad_attend])
    grad_heads = jnp.concatenate(
        [
            jnp.dot(
                attend_rows[stream], weights[1][stream], preferred_element_type=jnp.float32
            ).astype(jnp.bfloat16)
            for stream in range(2)
        ]
    )
    grad_columns = attend_back(columns, attended, logsum, grad_heads, heads_local)
    column_rows = [grad_columns[:split], grad_columns[split:]]
    column_sums = [
        jnp.sum(column_rows[stream], 0, dtype=jnp.float32).reshape(heads_local, 3, HEAD_DIM)
        for stream in range(2)
    ]
    text_place = split // attend_rows[1].shape[0]

    def factors(columns):
        return [
            (attend_rows[0], attended, 0),
            (attend_rows[1], attended, text_place),
            (joined[0], columns, 0),
            (joined[1], columns, text_place),
        ]

    if pending:
        grad_attention = weight_grads(factors(grad_columns))
        column_rows = after(column_rows, grad_attention)
        summed, _ = scatter_streams(column_rows, weights[0])
    else:
        summed, started = scatter_streams(column_rows, weights[0])
        grad_attention = weight_grads(factors(after(grad_columns, started)))
        summed = after(summed, grad_attention)
    grad_attention = scatter_weights(grad_attention)
    tensor_rank = lax.axis_index("tensor")
    width_local = heads_local * HEAD_DIM
    hidden_local = preact[0].shape[1]

    def placed(length, values, offset):
        return lax.dynamic_update_slice_in_dim(
            jnp.zeros((length,), jnp.float32), values, offset, 0
        )

    new_grads, slot_grads, bias_grads = ([], [], [])
    for stream in range(2):
        shift_back = jax.vjp(modulate, states[stream], shifts[stream][0], shifts[stream][1])[1]
        back_rows, back_shift, back_scale = shift_back(summed[stream])
        new_grads.append(grad_middle[stream] + back_rows)
        slot_grad = jnp.concatenate(
            [
                back_shift,
                back_scale,
                gate_attend[stream],
                shift_feed[stream],
                scale_feed[stream],
                gate_feed[stream],
            ]
        )
        slot_grads.append(slot_grad)
        bias_grads.append(
            jnp.concatenate(
                [
                    slot_grad,
                    placed(D, column_sums[stream][:, 0].reshape(-1), tensor_rank * width_local),
                    placed(D, column_sums[stream][:, 2].reshape(-1), tensor_rank * width_local),
                    jnp.sum(grad_attend[stream], 0),
                    placed(FF, hidden_sums[stream], tensor_rank * hidden_local),
                    jnp.sum(grad_branch[stream], 0),
                ]
            )
        )
    out_width = attended.shape[1]
    layer_grads = (
        unpack_weights(grad_attention, 2 * out_width, 3 * out_width),
        unpack_weights(grad_attention, 0, out_width),
        unpack_weights(grad_expansion, 0, hidden_local),
        unpack_weights(grad_contraction, 0, hidden_local),
    )
    pending = (grad_contraction, grad_expansion, grad_attention)
    return (
        new_grads,
        layer_grads,
        pending,
        jnp.stack(bias_grads),
        jnp.stack(slot_grads),
    )


def slot_table(silu_rows, modulation, slots):
    size = lax.axis_size("tensor")
    rank = lax.axis_index("tensor")
    count = silu_rows.shape[0]
    partial = jnp.einsum(
        "nd,lsdm->nlsm", silu_rows, modulation.astype(jnp.float32), precision=highest
    ).reshape(count, -1)
    width = partial.shape[1] // size
    owned = 0.0
    for step in range(size):
        block = lax.dynamic_slice_in_dim(partial, (rank ^ step) * width, width, 1)
        owned = owned + (exchange(block, "tensor", step) if step else block)
    onehot = (slots[:, None] == jnp.arange(count, dtype=jnp.int32)[None, :]).astype(jnp.float32)
    per_slot = jnp.dot(onehot, owned, precision=highest)
    mine = per_slot[0]
    for step in range(1, per_slot.shape[0]):
        mine = mine + exchange(per_slot[step], "dp", step)
    table = jnp.zeros((partial.shape[1],), jnp.float32)
    for step, block in enumerate(gather_parts(mine, "tensor")):
        table = lax.dynamic_update_slice_in_dim(table, block, (rank ^ step) * width, 0)
    return table.reshape(LAYERS, 2, -1)


def gather_slots(slot_grads):
    size = lax.axis_size("tensor")
    rank = lax.axis_index("tensor")
    values = slot_grads.reshape(size, 1, -1)
    owned = lax.dynamic_index_in_dim(values, rank, 0, False)
    for step in range(1, size):
        block = lax.dynamic_index_in_dim(values, rank ^ step, 0, False)
        owned = owned + exchange(block, "tensor", step)
    owned = gather_rows(owned, "dp")
    result = jnp.zeros((owned.shape[0], size * owned.shape[1]), jnp.float32)
    for step, block in enumerate(gather_parts(owned, "tensor")):
        result = lax.dynamic_update_slice_in_dim(result, block, (rank ^ step) * owned.shape[1], 1)
    return result


def on_device(
    image_tokens,
    text_tokens,
    conditioning,
    slot_sequence,
    rank_counts,
    projection,
    recombine,
    expansion,
    contraction,
    modulation,
    biases,
    cotangent_image,
    cotangent_text,
):
    tensor_rank = lax.axis_index("tensor")
    flat_rank = lax.axis_index(("dp", "tensor"))
    heads_local = HEADS // lax.axis_size("tensor")
    width_local = heads_local * HEAD_DIM
    hidden_local = FF // lax.axis_size("tensor")
    bias_all = gather_biases(biases)
    shard_rows = modulation.shape[2]
    owned_rows = lax.dynamic_slice_in_dim(
        jax.nn.silu(conditioning), flat_rank * shard_rows, shard_rows, 1
    )
    slots = jnp.concatenate(gather_parts(slot_sequence, "dp"))
    slot_shifts = slot_table(owned_rows, modulation, slots) + bias_all[:, :, : 6 * D]
    live = (rank_counts[0] > 0).astype(jnp.float32)
    states = [image_tokens.astype(jnp.float32), text_tokens.astype(jnp.float32)]
    stored = []
    for tier in range(LAYERS):
        attention, up, down = [
            lax.all_gather(matrix, "dp", axis=1, tiled=True)
            for matrix in (
                jnp.concatenate([projection[tier], recombine[tier]], axis=2),
                expansion[tier],
                contraction[tier],
            )
        ]
        width = projection.shape[3]
        weights = [attention[:, :, :width], attention[:, :, width:], up, down]
        pieces = layer_biases(bias_all[tier], tensor_rank, width_local, hidden_local)
        shifts = [
            [slot_shifts[tier, stream, part * D : (part + 1) * D] for part in range(6)]
            for stream in range(2)
        ]
        record, states = forward_layer(states, weights, pieces, shifts, heads_local)
        stored.append((weights, shifts, record))
    gradients = [
        cotangent_image.astype(jnp.float32) * live,
        cotangent_text.astype(jnp.float32) * live,
    ]
    slot_rows = jnp.dot(
        (
            slots[:, None] == jnp.arange(conditioning.shape[0], dtype=jnp.int32)[None, :]
        ).astype(jnp.float32),
        owned_rows,
        precision=highest,
    )
    weight_store, bias_store, slot_store, pending = ([], [], [], ())
    for tier in reversed(range(LAYERS)):
        weights, shifts, record = stored[tier]
        gradients, layer_grads, pending, bias_part, slot_grads = backward_layer(
            gradients, record, weights, shifts, heads_local, pending
        )
        weight_store.insert(0, layer_grads)
        bias_store.insert(0, bias_part)
        slot_store.insert(0, slot_grads)
    slot_sums = gather_slots(jnp.stack(slot_store, axis=1))
    modulation_grad = (
        jnp.dot(slot_rows.T, slot_sums, precision=highest)
        .reshape(shard_rows, 2, LAYERS, -1)
        .transpose(2, 1, 0, 3)
    )
    stacked = [
        jnp.stack([entry[kind] for entry in weight_store]) for kind in range(4)
    ]
    biases_grad = scatter_biases(jnp.stack(bias_store), biases.shape[2])
    return (
        (states[0] * live).astype(jnp.bfloat16),
        (states[1] * live).astype(jnp.bfloat16),
        gradients[0],
        gradients[1],
        stacked[0],
        stacked[1],
        stacked[2],
        stacked[3],
        modulation_grad,
        biases_grad,
    )


def solution(mesh):
    in_specs = (
        P(("dp", "tensor"), None),
        P(("dp", "tensor"), None),
        P(),
        P("dp"),
        P("dp"),
        P(None, None, "dp", "tensor"),
        P(None, None, "dp", "tensor"),
        P(None, None, "dp", "tensor"),
        P(None, None, "dp", "tensor"),
        P(None, None, ("dp", "tensor"), None),
        P(None, None, ("dp", "tensor")),
        P(("dp", "tensor"), None),
        P(("dp", "tensor"), None),
    )
    out_specs = (
        P(("dp", "tensor"), None),
        P(("dp", "tensor"), None),
        P(("dp", "tensor"), None),
        P(("dp", "tensor"), None),
        P(None, None, "dp", "tensor"),
        P(None, None, "dp", "tensor"),
        P(None, None, "dp", "tensor"),
        P(None, None, "dp", "tensor"),
        P(None, None, ("dp", "tensor"), None),
        P(None, None, ("dp", "tensor")),
    )
    return jax.shard_map(
        on_device, mesh=mesh, in_specs=in_specs, out_specs=out_specs, check_vma=False
    )
```
